512 devices in a mesh: plane: 16 (over x, z_hi), tile: 32 (over z_lo, y, core).
Axes of the slice: x: 4, y: 4, z: 16 (z_hi: 4, z_lo: 4; z = z_hi * 4 + z_lo), core: 2. Of those that a mesh axis runs over, the one named last changes fastest.
Arguments:
- density: float32 [48, 256, 2048], P('plane', 'tile'), may hold values from -6 to 6
- plane_slot: int32 [48], replicated, may hold values from 0 to 95, as said below
- paint_weight: float32 [32, 9], replicated, may hold values from -2 to 2
- paint_bias: float32 [32], replicated, may hold values from -0.5 to 0.5
- mix_weight: float32 [32], replicated, may hold values from -1 to 1
- short_kernel: float32 [5, 5], replicated, may hold values from -1 to 1
Outputs:
- distortion: float32 [4, 48, 256, 2048], P(None, 'plane', 'tile')
The draws below stay inside these ranges and needn't reach their ends.
Inputs may be any that keep to these rules, and one draw needn't show every extreme that they name: `plane_slot`: strictly increasing along the planes; the first is 0 and the last is 95.
All inputs are finite; a program needn't handle non-finite values.
Results may differ from the reference program's by a relative error of at most 0.00026.
Values sent between devices are 32-bit elements; how exact they have to be, the bound alone decides.
No kernel may reach another device: no remote copies, remote signals or barrier semaphores. Data moves between devices by JAX's collectives and lax.ppermute only.
A program may use at most 64 MiB of HBM per device.

```python
import math
import jax
import jax.numpy as jnp
from jax import lax

TR = 8
NC = 2048
CH = 32
NPL = 48
NR = 256
SLOTS = 96
N_TILE = 32


def draw_density(key, part):
    values = jnp.clip(jax.random.normal(key, (NPL, NR, NC), jnp.float32), -6.0, 6.0)
    return values


def draw_plane_slot(key, part):
    inner = 1 + jax.random.permutation(key, SLOTS - 2)[:NPL - 2]
    chosen = jnp.concatenate([jnp.zeros((1,), jnp.int32), inner.astype(jnp.int32), jnp.full((1,), SLOTS - 1, jnp.int32)])
    return jnp.sort(chosen)


def scatter_about(rng, extent, deviation, bound, kind=jnp.bfloat16):
    return jnp.clip(deviation * jax.random.normal(rng, extent, jnp.float32), -bound, bound).astype(kind)


def setup_inputs(seed: int = 0) -> dict:
    arg_keys = jax.random.split(jax.random.key(seed), 7)
    return {
        "density": draw_density(jax.random.fold_in(arg_keys[6], 71), 0),
        "plane_slot": draw_plane_slot(jax.random.fold_in(arg_keys[6], 71), 0),
        "paint_weight": scatter_about(arg_keys[2], (CH, 9), 9 ** -0.5, 2.0, jnp.float32),
        "paint_bias": jnp.clip(jax.random.uniform(arg_keys[3], (CH,), jnp.float32, -0.5, 0.5), -0.5, 0.5),
        "mix_weight": scatter_about(arg_keys[4], (CH,), CH ** -0.5, 1.0, jnp.float32),
        "short_kernel": scatter_about(arg_keys[5], (5, 5), 0.2, 1.0, jnp.float32),
    }


highest = lax.Precision.HIGHEST
lens_gain = 0.25

def paint_rows(extended, paint_weight, paint_bias, mix_weight):
    row_count = extended.shape[-2] - 4
    col_count = extended.shape[-1]
    padded = jnp.pad(extended, [(0, 0)] * (extended.ndim - 1) + [(2, 2)])
    stacked = jnp.stack([padded[..., 2 + 2 * row_step:2 + 2 * row_step + row_count, 2 + 2 * col_step:2 + 2 * col_step + col_count] for row_step in (-1, 0, 1) for col_step in (-1, 0, 1)], axis=0)
    before = jnp.einsum('ct,t...->c...', paint_weight, stacked, precision=highest)
    hidden = jnp.tanh(before + paint_bias.reshape((-1,) + (1,) * (before.ndim - 1)))
    return jnp.einsum('c,c...->...', mix_weight, hidden, precision=highest)

def short_rows(extended, short_kernel):
    row_count = extended.shape[-2] - 4
    col_count = extended.shape[-1]
    padded = jnp.pad(extended, [(0, 0)] * (extended.ndim - 1) + [(2, 2)])
    running = jnp.zeros(extended.shape[:-2] + (row_count, col_count), jnp.float32)
    for row_tap in range(5):
        for col_tap in range(5):
            running = running + short_kernel[row_tap, col_tap] * padded[..., row_tap:row_tap + row_count, col_tap:col_tap + col_count]
    return running

def hessian_rows(extended):
    padded = jnp.pad(extended, [(0, 0)] * (extended.ndim - 1) + [(1, 1)])
    center = padded[..., 1:-1, 1:-1]
    second_rows = padded[..., 2:, 1:-1] - 2.0 * center + padded[..., :-2, 1:-1]
    second_cols = padded[..., 1:-1, 2:] - 2.0 * center + padded[..., 1:-1, :-2]
    mixed_part = (padded[..., 2:, 2:] - padded[..., 2:, :-2] - padded[..., :-2, 2:] + padded[..., :-2, :-2]) * 0.25
    return jnp.stack([second_rows, second_cols, mixed_part], axis=0)

def lens_step(lens_state, shear_field, mixing, bending):
    previous = lens_state[0:2]
    current = lens_state[2:4]
    bent_first = shear_field[0] * current[0] + shear_field[2] * current[1]
    bent_second = shear_field[2] * current[0] + shear_field[1] * current[1]
    bent_rows = jnp.stack([bent_first, bent_second], axis=0)
    advanced = (1.0 - mixing) * previous + mixing * current - bending * bent_rows
    return jnp.concatenate([current, advanced], axis=0)

def distances(plane_slot, slot_total):
    distance = (plane_slot.astype(jnp.float32) + 1.0) / slot_total
    before = jnp.concatenate([jnp.zeros((1,), jnp.float32), distance[:-1]])
    after = jnp.concatenate([distance[1:], jnp.full((1,), (slot_total + 1.0) / slot_total, jnp.float32)])
    mixing = before * (after - distance) / (distance * (after - before))
    bending = lens_gain * (after - distance) / after
    return (mixing, bending)

def coarse_kernel(row_global, col_global, scale):
    gap = row_global.astype(jnp.float32)[:, None] - col_global.astype(jnp.float32)[None, :]
    return jnp.exp(-jnp.abs(gap) / scale)

def reference(density, plane_slot, paint_weight, paint_bias, mix_weight, short_kernel):
    total_rows = TR * N_TILE
    coarse_rows = total_rows // 4
    coarse_cols = NC // 4
    row_scale = total_rows / 16.0
    col_scale = NC / 16.0
    long_gain = 1.0 / math.sqrt(row_scale * col_scale)
    row_kernel = coarse_kernel(jnp.arange(coarse_rows, dtype=jnp.int32), jnp.arange(coarse_rows, dtype=jnp.int32), row_scale)
    col_kernel = coarse_kernel(jnp.arange(coarse_cols, dtype=jnp.int32), jnp.arange(coarse_cols, dtype=jnp.int32), col_scale)
    mixing, bending = distances(plane_slot, SLOTS)

    def one_plane(lens_state, inputs):
        plane_map, mixing_here, bending_here = inputs
        convergence = paint_rows(jnp.pad(plane_map, ((2, 2), (0, 0))), paint_weight, paint_bias, mix_weight)
        short_part = short_rows(jnp.pad(convergence, ((2, 2), (0, 0))), short_kernel)
        coarse = convergence.reshape(coarse_rows, 4, coarse_cols, 4).mean(axis=(1, 3))
        long_part = long_gain * jnp.dot(jnp.dot(row_kernel, coarse, precision=highest), col_kernel, precision=highest)
        potential = short_part + jnp.repeat(jnp.repeat(long_part, 4, axis=0), 4, axis=1)
        shear_field = hessian_rows(jnp.pad(potential, ((1, 1), (0, 0))))
        lens_state = lens_step(lens_state, shear_field, mixing_here, bending_here)
        return (lens_state, lens_state[2:4].reshape(4, total_rows, NC))
    pattern = jnp.array([[1.0, 0.0], [0.0, 1.0], [1.0, 0.0], [0.0, 1.0]], jnp.float32)
    start_state = jnp.broadcast_to(pattern[:, :, None, None], (4, 2, total_rows, NC)).astype(jnp.float32)
    unused_state, results = lax.scan(one_plane, start_state, (density, mixing, bending))
    return jnp.transpose(results, (1, 0, 2, 3))
```

```python
import functools
import math

import jax
import jax.numpy as jnp
from jax import lax
from jax.experimental import pallas as pl
from jax.experimental.pallas import tpu as pltpu
from jax.sharding import PartitionSpec as P

f32 = jnp.float32
bf16 = jnp.bfloat16
lens_gain = 0.25
channels = 32
highest = lax.Precision.HIGHEST


def distances(plane_slot, slot_total):
    distance = (plane_slot.astype(f32) + 1.0) / slot_total
    before = jnp.concatenate([jnp.zeros((1,), f32), distance[:-1]])
    after = jnp.concatenate([distance[1:], jnp.full((1,), (slot_total + 1.0) / slot_total, f32)])
    mixing = before * (after - distance) / (distance * (after - before))
    bending = lens_gain * (after - distance) / after
    return (mixing, bending)


def shifted(value, by):
    width = value.shape[-1]
    rolled = pltpu.roll(value, (-by) % width, value.ndim - 1)
    lane = lax.broadcasted_iota(jnp.int32, value.shape, value.ndim - 1)
    keep = lane < width - by if by > 0 else lane >= -by
    return jnp.where(keep, rolled, 0.0)


def paint_matrix(paint_weight, paint_bias):
    high = lax.reduce_precision(paint_weight, 8, 7)
    low = lax.reduce_precision(paint_weight - high, 8, 7)
    bias_0 = lax.reduce_precision(paint_bias, 8, 7)
    bias_1 = lax.reduce_precision(paint_bias - bias_0, 8, 7)
    bias_2 = paint_bias - bias_0 - bias_1
    spread = lambda value: jnp.repeat(value, 8, axis=0)
    high, low = spread(high), spread(low)
    shape = (channels * 8, 160)
    row = lax.broadcasted_iota(jnp.int32, shape, 0) % 8
    col = lax.broadcasted_iota(jnp.int32, shape, 1)
    part, in_row = col // 16, col % 16
    total = jnp.zeros(shape, f32)
    for i in range(3):
        for j in range(3):
            here = (in_row == row + 2 * i) & (part % 3 == j) & (part < 9)
            tap = 3 * i + j
            value = jnp.where(part < 6, high[:, tap : tap + 1], low[:, tap : tap + 1])
            total = jnp.where(here, value, total)
    for k, value in enumerate((bias_0, bias_1, bias_2)):
        total = jnp.where(col == 144 + k, spread(value[:, None]), total)
    return total.astype(bf16)


def paint_kernel(edge_ref, mix_ref, x_ref, low_ref, high_ref, w_ref, pool_ref, c_ref, coarse_ref, wide, stack, sums):
    cols = x_ref.shape[-1]
    wide[...] = jnp.zeros_like(wide)
    sums[...] = jnp.zeros_like(sums)
    stack[144:160, :] = jnp.ones((16, cols), bf16)
    first = edge_ref[0] == 0
    last = edge_ref[1] == 0
    row = lax.broadcasted_iota(jnp.int32, (8, 256), 0)
    for p in range(3):
        wide[0, 0:5, :] = low_ref[p]
        wide[0, 5:13, :] = x_ref[p]
        wide[1, 0:7, :] = x_ref[p, 1:8, :]
        wide[1, 7:12, :] = high_ref[p]
        for window in range(2):
            value = wide[window]
            for j in range(3):
                moved = value if j == 1 else shifted(value, 2 * (j - 1))
                upper = moved.astype(bf16)
                lower = (moved - upper.astype(f32)).astype(bf16)
                stack[16 * j : 16 * j + 16, :] = upper
                stack[48 + 16 * j : 64 + 16 * j, :] = lower
                stack[96 + 16 * j : 112 + 16 * j, :] = upper

            def one_chunk(chunk, carry):
                at = pl.ds(pl.multiple_of(chunk * 256, 256), 256)
                before = jnp.dot(w_ref[...], stack[:, at], preferred_element_type=f32)
                total = jnp.zeros((8, 256), f32)
                for c in range(channels):
                    total = total + mix_ref[c] * jnp.tanh(before[8 * c : 8 * c + 8, :])
                if window == 0:
                    total = jnp.where(first & (row < 3), 0.0, total)
                    c_ref[p, 0:8, at] = total
                else:
                    total = jnp.where(last & (row >= 5), 0.0, total)
                    c_ref[p, 8:14, at] = total[2:8]
                return carry

            lax.fori_loop(0, cols // 256, one_chunk, 0)
        value = c_ref[p, 3:11, :]
        sums[p : p + 1, :] = jnp.sum(value[0:4], axis=0, keepdims=True)
        sums[3 + p : 4 + p, :] = jnp.sum(value[4:8], axis=0, keepdims=True)
    c_ref[:, 14:16, :] = jnp.zeros((3, 2, cols), f32)
    quarter = cols // 4
    stacked = jnp.concatenate([sums[:, quarter * v : quarter * (v + 1)] for v in range(4)], axis=0)
    pooled = jnp.dot(stacked, pool_ref[...], precision=highest, preferred_element_type=f32)
    for v in range(4):
        coarse_ref[:, 128 * v : 128 * v + 128] = pooled[8 * v : 8 * v + 8]


def short_kernel_body(k_ref, c_ref, s_ref, held):
    cols = c_ref.shape[-1]
    for p in range(3):
        held[0:16, :] = c_ref[p]
        held[16:24, :] = jnp.zeros((8, cols), f32)
        for window in range(2):
            total = jnp.zeros((8, cols), f32)
            for b in range(5):
                part = jnp.zeros((8, cols), f32)
                for a in range(5):
                    start = 8 * window + a
                    part = part + k_ref[5 * a + b] * held[start : start + 8, :]
                total = total + (part if b == 2 else shifted(part, b - 2))
            s_ref[p, 8 * window : 8 * window + 8, :] = total


def bend_kernel(decay, gain, edge_ref, s_ref, coarse_ref, acc_ref, ec_ref, grow_ref, u_ref, rows, pot):
    cols = s_ref.shape[-1]
    e = decay
    c0, c1 = coarse_ref[0:3, :], coarse_ref[3:6, :]
    up, down = acc_ref[0:3, :], acc_ref[3:6, :]
    rows[12:16, :] = jnp.zeros((4, rows.shape[-1]), f32)
    rows[0:3, :] = e * c0 + e * e * c1 + e * e * down + up * (1.0 / e)
    rows[3:6, :] = c0 + e * c1 + up + e * down
    rows[6:9, :] = c1 + e * c0 + e * up + down
    rows[9:12, :] = e * e * c0 + e * c1 + e * e * up + down * (1.0 / e)
    smooth = gain * jnp.dot(rows[...], ec_ref[...], precision=highest, preferred_element_type=f32)
    stacked = jnp.concatenate([smooth[:, 128 * v : 128 * v + 128] for v in range(4)], axis=0)
    grown = jnp.dot(stacked, grow_ref[...], precision=highest, preferred_element_type=f32)
    long = jnp.concatenate([grown[16 * v : 16 * v + 16] for v in range(4)], axis=1)
    row = lax.broadcasted_iota(jnp.int32, (8, cols), 0)
    top = edge_ref[0] != 0
    bottom = edge_ref[1] != 0
    for p in range(3):
        part = s_ref[p]
        wide = jnp.where(
            row < 4,
            jnp.broadcast_to(long[3 + p : 4 + p], (8, cols)),
            jnp.broadcast_to(long[6 + p : 7 + p], (8, cols)),
        )
        here = part[1:9] + wide
        pot[7:8, :] = jnp.where(top, part[0:1] + long[p : p + 1], 0.0)
        pot[8:16, :] = here
        pot[16:17, :] = jnp.where(bottom, part[9:10] + long[9 + p : 10 + p], 0.0)
        above, below = pot[7:15, :], pot[9:17, :]
        u11 = below - 2.0 * here + above
        u22 = shifted(here, 1) - 2.0 * here + shifted(here, -1)
        step = below - above
        u12 = (shifted(step, 1) - shifted(step, -1)) * 0.25
        for d in range(cols // 128):
            at = slice(128 * d, 128 * d + 128)
            u_ref[9 * d + 3 * p] = u11[:, at]
            u_ref[9 * d + 3 * p + 1] = u12[:, at]
            u_ref[9 * d + 3 * p + 2] = u22[:, at]


def advance(previous, current, u11, u12, u22, mixing, bending):
    kept = 1.0 - mixing
    bent = (
        u11 * current[0] + u12 * current[2],
        u11 * current[1] + u12 * current[3],
        u12 * current[0] + u22 * current[2],
        u12 * current[1] + u22 * current[3],
    )
    return tuple(kept * previous[i] + mixing * current[i] - bending * bent[i] for i in range(4))


def scan_kernel(mixing_ref, bending_ref, u_ref, state_ref):
    one = jnp.ones((8, 128), f32)
    zero = jnp.zeros((8, 128), f32)
    groups = u_ref.shape[0] // 9

    def one_group(g, carry):
        previous, current = carry
        for i in range(4):
            state_ref[8 * g + i] = previous[i]
            state_ref[8 * g + 4 + i] = current[i]
        for p in range(3):
            at = 9 * g + 3 * p
            k = 3 * g + p
            later = advance(previous, current, u_ref[at], u_ref[at + 1], u_ref[at + 2], mixing_ref[k], bending_ref[k])
            previous, current = current, later
        return (previous, current)

    start = (one, zero, zero, one)
    lax.fori_loop(0, groups, one_group, (start, start))


def final_kernel(mixing_ref, bending_ref, u_ref, state_ref, out_ref):
    blocks = u_ref.shape[0] // 9

    def one_block(d, carry):
        at = pl.ds(pl.multiple_of(d * 128, 128), 128)
        previous = tuple(state_ref[8 * d + i] for i in range(4))
        current = tuple(state_ref[8 * d + 4 + i] for i in range(4))
        for p in range(3):
            k = 9 * d + 3 * p
            later = advance(
                previous, current, u_ref[k], u_ref[k + 1], u_ref[k + 2], mixing_ref[p], bending_ref[p]
            )
            for i in range(4):
                out_ref[i, p, :, at] = later[i]
            previous, current = current, later
        return carry

    lax.fori_loop(0, blocks, one_block, 0)


vmem = pl.BlockSpec(memory_space=pltpu.VMEM)
smem = pl.BlockSpec(memory_space=pltpu.SMEM)


def sds(*shape):
    return jax.ShapeDtypeStruct(shape, f32)


def call(kernel, name, n_smem, n_vmem, out_shape, scratch=(), cost=(0, 0, 0)):
    outs = jax.tree.map(lambda _: vmem, out_shape)
    return pl.pallas_call(
        kernel,
        name=name,
        out_shape=out_shape,
        in_specs=[smem] * n_smem + [vmem] * n_vmem,
        out_specs=outs,
        scratch_shapes=list(scratch),
        cost_estimate=pl.CostEstimate(flops=cost[0], bytes_accessed=cost[1], transcendentals=cost[2]),
        compiler_params=pltpu.CompilerParams(vmem_limit_bytes=24 << 20),
    )


def row_scan(message, tile_index, tile_count):
    row = lax.broadcasted_iota(jnp.int32, (8, 1), 0)
    forward = row < 3
    block = message
    total = jnp.zeros_like(message)
    size = 1
    while size < tile_count:
        received = lax.ppermute(block, "tile", [(i, i ^ size) for i in range(tile_count)])
        from_lower = (tile_index & size) != 0
        place = (tile_index % size).astype(f32)
        weight = jnp.where(forward, jnp.exp(-place / 8.0), jnp.exp(-(size - 1 - place) / 8.0))
        used = forward == from_lower
        total = total + jnp.where(used, weight, 0.0) * received
        far = math.exp(-size / 8.0)
        block = jnp.where(used, block + far * received, far * block + received)
        size *= 2
    return total


def body(density, plane_slot, paint_weight, paint_bias, mix_weight, short_kernel):
    plane_count, row_count, col_count = density.shape
    tile_count = lax.axis_size("tile")
    group_count = lax.axis_size("plane")
    tile_index = lax.axis_index("tile")
    plane_index = lax.axis_index("plane")
    coarse_cols = col_count // 4
    row_scale = row_count * tile_count / 16.0
    col_scale = col_count / 16.0
    long_gain = 1.0 / math.sqrt(row_scale * col_scale)
    decay = math.exp(-1.0 / row_scale)

    up = [(i, i + 1) for i in range(tile_count - 1)]
    low = lax.ppermute(density[:, 3:8, :], "tile", up)
    high = lax.ppermute(density[:, 0:5, :], "tile", [(b, a) for a, b in up])

    edge = jnp.stack([tile_index, tile_count - 1 - tile_index]).astype(jnp.int32)
    mixing, bending = distances(plane_slot, 2 * plane_slot.shape[0])
    mixing_here = lax.dynamic_slice_in_dim(mixing, plane_index * plane_count, plane_count)
    bending_here = lax.dynamic_slice_in_dim(bending, plane_index * plane_count, plane_count)
    weights = paint_matrix(paint_weight, paint_bias)
    gap = lax.broadcasted_iota(jnp.int32, (coarse_cols, coarse_cols), 0) - lax.broadcasted_iota(
        jnp.int32, (coarse_cols, coarse_cols), 1
    )
    col_kernel = jnp.exp(-jnp.abs(gap.astype(f32)) / col_scale)
    pool = jnp.where(
        lax.broadcasted_iota(jnp.int32, (512, 128), 0) // 4 == lax.broadcasted_iota(jnp.int32, (512, 128), 1),
        1.0 / 16.0,
        0.0,
    ).astype(f32)
    grow = jnp.where(
        lax.broadcasted_iota(jnp.int32, (128, 512), 1) // 4 == lax.broadcasted_iota(jnp.int32, (128, 512), 0), 1.0, 0.0
    ).astype(f32)

    convergence, coarse = call(
        paint_kernel,
        "paint",
        2,
        5,
        (sds(3, 16, col_count), sds(8, coarse_cols)),
        [pltpu.VMEM((2, 16, col_count), f32), pltpu.VMEM((160, col_count), bf16), pltpu.VMEM((8, col_count), f32)],
        (8 * 10**9, 2 * 10**6, 10**6),
    )(edge, mix_weight, density, low, high, weights, pool)

    e = decay
    c0, c1 = coarse[0:3], coarse[3:6]
    message = jnp.concatenate([e * e * c0 + e * c1, e * c0 + e * e * c1, jnp.zeros_like(coarse[0:2])], axis=0)
    received = row_scan(message, tile_index, tile_count)

    short_part = call(
        short_kernel_body,
        "short",
        1,
        1,
        sds(3, 16, col_count),
        [pltpu.VMEM((24, col_count), f32)],
        (10**7, 10**6, 0),
    )(short_kernel.reshape(25), convergence)

    shear = call(
        functools.partial(bend_kernel, decay, long_gain),
        "bend",
        1,
        5,
        sds(group_count * 9, 8, 128),
        [pltpu.VMEM((16, coarse_cols), f32), pltpu.VMEM((24, col_count), f32)],
        (10**8, 2 * 10**6, 0),
    )(edge, short_part, coarse, received, col_kernel, grow)

    gathered = lax.all_to_all(shear, "plane", 0, 0, tiled=True)
    states = call(scan_kernel, "scan", 2, 1, sds(group_count * 8, 8, 128), (), (10**7, 10**6, 0))(
        mixing, bending, gathered
    )
    mine = lax.all_to_all(states, "plane", 0, 0, tiled=True)
    return call(final_kernel, "final", 2, 2, sds(4, plane_count, row_count, col_count), (), (10**7, 10**6, 0))(
        mixing_here, bending_here, shear, mine
    )


def solution(mesh):
    placed = (P("plane", "tile", None), P(), P(), P(), P(), P())
    return jax.shard_map(
        body, mesh=mesh, in_specs=placed, out_specs=P(None, "plane", "tile", None), check_vma=False
    )
```

```python
import functools
import math

import jax
import jax.numpy as jnp
from jax import lax
from jax.experimental import pallas as pl
from jax.experimental.pallas import tpu as pltpu
from jax.sharding import PartitionSpec as P

f32 = jnp.float32
bf16 = jnp.bfloat16
lens_gain = 0.25
channels = 32
highest = lax.Precision.HIGHEST


def distances(plane_slot, slot_total):
    distance = (plane_slot.astype(f32) + 1.0) / slot_total
    before = jnp.concatenate([jnp.zeros((1,), f32), distance[:-1]])
    after = jnp.concatenate([distance[1:], jnp.full((1,), (slot_total + 1.0) / slot_total, f32)])
    mixing = before * (after - distance) / (distance * (after - before))
    bending = lens_gain * (after - distance) / after
    return (mixing, bending)


def shifted(value, by):
    width = value.shape[-1]
    rolled = pltpu.roll(value, (-by) % width, value.ndim - 1)
    lane = lax.broadcasted_iota(jnp.int32, value.shape, value.ndim - 1)
    keep = lane < width - by if by > 0 else lane >= -by
    return jnp.where(keep, rolled, 0.0)


def paint_matrix(paint_weight, paint_bias):
    high = lax.reduce_precision(paint_weight, 8, 7)
    low = lax.reduce_precision(paint_weight - high, 8, 7)
    bias_0 = lax.reduce_precision(paint_bias, 8, 7)
    bias_1 = lax.reduce_precision(paint_bias - bias_0, 8, 7)
    bias_2 = paint_bias - bias_0 - bias_1
    spread = lambda value: jnp.repeat(value, 8, axis=0)
    high, low = spread(high), spread(low)
    shape = (channels * 8, 160)
    row = lax.broadcasted_iota(jnp.int32, shape, 0) % 8
    col = lax.broadcasted_iota(jnp.int32, shape, 1)
    part, in_row = col // 16, col % 16
    total = jnp.zeros(shape, f32)
    for i in range(3):
        for j in range(3):
            here = (in_row == row + 2 * i) & (part % 3 == j) & (part < 9)
            tap = 3 * i + j
            value = jnp.where(part < 6, high[:, tap : tap + 1], low[:, tap : tap + 1])
            total = jnp.where(here, value, total)
    for k, value in enumerate((bias_0, bias_1, bias_2)):
        total = jnp.where(col == 144 + k, spread(value[:, None]), total)
    return total.astype(bf16)


def paint_kernel(edge_ref, mix_ref, x_ref, low_ref, high_ref, w_ref, pool_ref, c_ref, coarse_ref, wide, stack, sums):
    cols = x_ref.shape[-1]
    wide[...] = jnp.zeros_like(wide)
    sums[...] = jnp.zeros_like(sums)
    stack[144:160, :] = jnp.ones((16, cols), bf16)
    first = edge_ref[0] == 0
    last = edge_ref[1] == 0
    row = lax.broadcasted_iota(jnp.int32, (8, 256), 0)
    for p in range(3):
        wide[0, 0:5, :] = low_ref[p]
        wide[0, 5:13, :] = x_ref[p]
        wide[1, 0:7, :] = x_ref[p, 1:8, :]
        wide[1, 7:12, :] = high_ref[p]
        for window in range(2):
            value = wide[window]
            for j in range(3):
                moved = value if j == 1 else shifted(value, 2 * (j - 1))
                upper = moved.astype(bf16)
                lower = (moved - upper.astype(f32)).astype(bf16)
                stack[16 * j : 16 * j + 16, :] = upper
                stack[48 + 16 * j : 64 + 16 * j, :] = lower
                stack[96 + 16 * j : 112 + 16 * j, :] = upper

            def one_chunk(chunk, carry):
                at = pl.ds(pl.multiple_of(chunk * 256, 256), 256)
                before = jnp.dot(w_ref[...], stack[:, at], preferred_element_type=f32)
                total = jnp.zeros((8, 256), f32)
                for c in range(channels):
                    total = total + mix_ref[c] * jnp.tanh(before[8 * c : 8 * c + 8, :])
                if window == 0:
                    total = jnp.where(first & (row < 3), 0.0, total)
                    c_ref[p, 0:8, at] = total
                else:
                    total = jnp.where(last & (row >= 5), 0.0, total)
                    c_ref[p, 8:14, at] = total[2:8]
                return carry

            lax.fori_loop(0, cols // 256, one_chunk, 0)
        value = c_ref[p, 3:11, :]
        sums[p : p + 1, :] = jnp.sum(value[0:4], axis=0, keepdims=True)
        sums[3 + p : 4 + p, :] = jnp.sum(value[4:8], axis=0, keepdims=True)
    c_ref[:, 14:16, :] = jnp.zeros((3, 2, cols), f32)
    quarter = cols // 4
    stacked = jnp.concatenate([sums[:, quarter * v : quarter * (v + 1)] for v in range(4)], axis=0)
    pooled = jnp.dot(stacked, pool_ref[...], precision=highest, preferred_element_type=f32)
    for v in range(4):
        coarse_ref[:, 128 * v : 128 * v + 128] = pooled[8 * v : 8 * v + 8]


def short_kernel_body(k_ref, c_ref, s_ref, held):
    cols = c_ref.shape[-1]
    for p in range(3):
        held[0:16, :] = c_ref[p]
        held[16:24, :] = jnp.zeros((8, cols), f32)
        for window in range(2):
            total = jnp.zeros((8, cols), f32)
            for b in range(5):
                part = jnp.zeros((8, cols), f32)
                for a in range(5):
                    start = 8 * window + a
                    part = part + k_ref[5 * a + b] * held[start : start + 8, :]
                total = total + (part if b == 2 else shifted(part, b - 2))
            s_ref[p, 8 * window : 8 * window + 8, :] = total


def bend_kernel(decay, gain, edge_ref, s_ref, coarse_ref, acc_ref, ec_ref, grow_ref, u_ref, rows, pot):
    cols = s_ref.shape[-1]
    e = decay
    c0, c1 = coarse_ref[0:3, :], coarse_ref[3:6, :]
    up, down = acc_ref[0:3, :], acc_ref[3:6, :]
    rows[12:16, :] = jnp.zeros((4, rows.shape[-1]), f32)
    rows[0:3, :] = e * c0 + e * e * c1 + e * e * down + up * (1.0 / e)
    rows[3:6, :] = c0 + e * c1 + up + e * down
    rows[6:9, :] = c1 + e * c0 + e * up + down
    rows[9:12, :] = e * e * c0 + e * c1 + e * e * up + down * (1.0 / e)
    smooth = gain * jnp.dot(rows[...], ec_ref[...], precision=highest, preferred_element_type=f32)
    stacked = jnp.concatenate([smooth[:, 128 * v : 128 * v + 128] for v in range(4)], axis=0)
    grown = jnp.dot(stacked, grow_ref[...], precision=highest, preferred_element_type=f32)
    long = jnp.concatenate([grown[16 * v : 16 * v + 16] for v in range(4)], axis=1)
    row = lax.broadcasted_iota(jnp.int32, (8, cols), 0)
    top = edge_ref[0] != 0
    bottom = edge_ref[1] != 0
    for p in range(3):
        part = s_ref[p]
        wide = jnp.where(
            row < 4,
            jnp.broadcast_to(long[3 + p : 4 + p], (8, cols)),
            jnp.broadcast_to(long[6 + p : 7 + p], (8, cols)),
        )
        here = part[1:9] + wide
        pot[7:8, :] = jnp.where(top, part[0:1] + long[p : p + 1], 0.0)
        pot[8:16, :] = here
        pot[16:17, :] = jnp.where(bottom, part[9:10] + long[9 + p : 10 + p], 0.0)
        above, below = pot[7:15, :], pot[9:17, :]
        u11 = below - 2.0 * here + above
        u22 = shifted(here, 1) - 2.0 * here + shifted(here, -1)
        step = below - above
        u12 = (shifted(step, 1) - shifted(step, -1)) * 0.25
        for d in range(cols // 128):
            at = slice(128 * d, 128 * d + 128)
            u_ref[9 * d + 3 * p] = u11[:, at]
            u_ref[9 * d + 3 * p + 1] = u12[:, at]
            u_ref[9 * d + 3 * p + 2] = u22[:, at]


def advance(previous, current, u11, u12, u22, mixing, bending):
    kept = 1.0 - mixing
    bent = (
        u11 * current[0] + u12 * current[2],
        u11 * current[1] + u12 * current[3],
        u12 * current[0] + u22 * current[2],
        u12 * current[1] + u22 * current[3],
    )
    return tuple(kept * previous[i] + mixing * current[i] - bending * bent[i] for i in range(4))


def scan_kernel(mixing_ref, bending_ref, u_ref, state_ref):
    one = jnp.ones((8, 128), f32)
    zero = jnp.zeros((8, 128), f32)
    groups = u_ref.shape[0] // 9

    def one_group(g, carry):
        previous, current = carry
        for i in range(4):
            state_ref[8 * g + i] = previous[i]
            state_ref[8 * g + 4 + i] = current[i]
        for p in range(3):
            at = 9 * g + 3 * p
            k = 3 * g + p
            later = advance(previous, current, u_ref[at], u_ref[at + 1], u_ref[at + 2], mixing_ref[k], bending_ref[k])
            previous, current = current, later
        return (previous, current)

    start = (one, zero, zero, one)
    lax.fori_loop(0, groups, one_group, (start, start))


def final_kernel(mixing_ref, bending_ref, u_ref, state_ref, out_ref):
    blocks = u_ref.shape[0] // 9

    def one_block(d, carry):
        at = pl.ds(pl.multiple_of(d * 128, 128), 128)
        previous = tuple(state_ref[8 * d + i] for i in range(4))
        current = tuple(state_ref[8 * d + 4 + i] for i in range(4))
        for p in range(3):
            k = 9 * d + 3 * p
            later = advance(
                previous, current, u_ref[k], u_ref[k + 1], u_ref[k + 2], mixing_ref[p], bending_ref[p]
            )
            for i in range(4):
                out_ref[i, p, :, at] = later[i]
            previous, current = current, later
        return carry

    lax.fori_loop(0, blocks, one_block, 0)


vmem = pl.BlockSpec(memory_space=pltpu.VMEM)
smem = pl.BlockSpec(memory_space=pltpu.SMEM)


def sds(*shape):
    return jax.ShapeDtypeStruct(shape, f32)


def call(kernel, name, n_smem, n_vmem, out_shape, scratch=(), cost=(0, 0, 0)):
    outs = jax.tree.map(lambda _: vmem, out_shape)
    return pl.pallas_call(
        kernel,
        name=name,
        out_shape=out_shape,
        in_specs=[smem] * n_smem + [vmem] * n_vmem,
        out_specs=outs,
        scratch_shapes=list(scratch),
        cost_estimate=pl.CostEstimate(flops=cost[0], bytes_accessed=cost[1], transcendentals=cost[2]),
        compiler_params=pltpu.CompilerParams(vmem_limit_bytes=24 << 20),
    )


def row_scan(message, tile_index, tile_count):
    row = lax.broadcasted_iota(jnp.int32, (8, 1), 0)
    forward = row < 3
    block = message
    total = jnp.zeros_like(message)
    size = 1
    while size < tile_count:
        received = lax.ppermute(block, "tile", [(i, i ^ size) for i in range(tile_count)])
        from_lower = (tile_index & size) != 0
        place = (tile_index % size).astype(f32)
        weight = jnp.where(forward, jnp.exp(-place / 8.0), jnp.exp(-(size - 1 - place) / 8.0))
        used = forward == from_lower
        total = total + jnp.where(used, weight, 0.0) * received
        far = math.exp(-size / 8.0)
        block = jnp.where(used, block + far * received, far * block + received)
        size *= 2
    return total


def body(density, plane_slot, paint_weight, paint_bias, mix_weight, short_kernel):
    plane_count, row_count, col_count = density.shape
    tile_count = lax.axis_size("tile")
    group_count = lax.axis_size("plane")
    tile_index = lax.axis_index("tile")
    plane_index = lax.axis_index("plane")
    coarse_cols = col_count // 4
    row_scale = row_count * tile_count / 16.0
    col_scale = col_count / 16.0
    long_gain = 1.0 / math.sqrt(row_scale * col_scale)
    decay = math.exp(-1.0 / row_scale)

    up = [(i, i + 1) for i in range(tile_count - 1)]
    low = lax.ppermute(density[:, 3:8, :], "tile", up)
    high = lax.ppermute(density[:, 0:5, :], "tile", [(b, a) for a, b in up])

    edge = jnp.stack([tile_index, tile_count - 1 - tile_index]).astype(jnp.int32)
    mixing, bending = distances(plane_slot, 2 * plane_slot.shape[0])
    mixing_here = lax.dynamic_slice_in_dim(mixing, plane_index * plane_count, plane_count)
    bending_here = lax.dynamic_slice_in_dim(bending, plane_index * plane_count, plane_count)
    weights = paint_matrix(paint_weight, paint_bias)
    gap = lax.broadcasted_iota(jnp.int32, (coarse_cols, coarse_cols), 0) - lax.broadcasted_iota(
        jnp.int32, (coarse_cols, coarse_cols), 1
    )
    col_kernel = jnp.exp(-jnp.abs(gap.astype(f32)) / col_scale)
    pool = jnp.where(
        lax.broadcasted_iota(jnp.int32, (512, 128), 0) // 4 == lax.broadcasted_iota(jnp.int32, (512, 128), 1),
        1.0 / 16.0,
        0.0,
    ).astype(f32)
    grow = jnp.where(
        lax.broadcasted_iota(jnp.int32, (128, 512), 1) // 4 == lax.broadcasted_iota(jnp.int32, (128, 512), 0), 1.0, 0.0
    ).astype(f32)

    convergence, coarse = call(
        paint_kernel,
        "paint",
        2,
        5,
        (sds(3, 16, col_count), sds(8, coarse_cols)),
        [pltpu.VMEM((2, 16, col_count), f32), pltpu.VMEM((160, col_count), bf16), pltpu.VMEM((8, col_count), f32)],
        (8 * 10**9, 2 * 10**6, 10**6),
    )(edge, mix_weight, density, low, high, weights, pool)
    coarse, convergence, mixing, bending, mixing_here, bending_here = lax.optimization_barrier(
        (coarse, convergence, mixing, bending, mixing_here, bending_here)
    )

    e = decay
    c0, c1 = coarse[0:3], coarse[3:6]
    message = jnp.concatenate([e * e * c0 + e * c1, e * c0 + e * e * c1, jnp.zeros_like(coarse[0:2])], axis=0)
    received = row_scan(message, tile_index, tile_count)

    short_part = call(
        short_kernel_body,
        "short",
        1,
        1,
        sds(3, 16, col_count),
        [pltpu.VMEM((24, col_count), f32)],
        (10**7, 10**6, 0),
    )(short_kernel.reshape(25), convergence)

    shear = call(
        functools.partial(bend_kernel, decay, long_gain),
        "bend",
        1,
        5,
        sds(group_count * 9, 8, 128),
        [pltpu.VMEM((16, coarse_cols), f32), pltpu.VMEM((24, col_count), f32)],
        (10**8, 2 * 10**6, 0),
    )(edge, short_part, coarse, received, col_kernel, grow)

    gathered = lax.all_to_all(shear, "plane", 0, 0, tiled=True)
    states = call(scan_kernel, "scan", 2, 1, sds(group_count * 8, 8, 128), (), (10**7, 10**6, 0))(
        mixing, bending, gathered
    )
    mine = lax.all_to_all(states, "plane", 0, 0, tiled=True)
    return call(final_kernel, "final", 2, 2, sds(4, plane_count, row_count, col_count), (), (10**7, 10**6, 0))(
        mixing_here, bending_here, shear, mine
    )


def solution(mesh):
    placed = (P("plane", "tile", None), P(), P(), P(), P(), P())
    return jax.shard_map(
        body, mesh=mesh, in_specs=placed, out_specs=P(None, "plane", "tile", None), check_vma=False
    )
```

```python
import functools
import math

import jax
import jax.numpy as jnp
from jax import lax
from jax.experimental import pallas as pl
from jax.experimental.pallas import tpu as pltpu
from jax.sharding import Mesh
from jax.sharding import PartitionSpec as P

f32 = jnp.float32
bf16 = jnp.bfloat16
lens_gain = 0.25
channels = 32
highest = lax.Precision.HIGHEST


def distances(plane_slot, slot_total):
    distance = (plane_slot.astype(f32) + 1.0) / slot_total
    before = jnp.concatenate([jnp.zeros((1,), f32), distance[:-1]])
    after = jnp.concatenate([distance[1:], jnp.full((1,), (slot_total + 1.0) / slot_total, f32)])
    mixing = before * (after - distance) / (distance * (after - before))
    bending = lens_gain * (after - distance) / after
    return (mixing, bending)


def shifted(value, by):
    width = value.shape[-1]
    rolled = pltpu.roll(value, (-by) % width, value.ndim - 1)
    lane = lax.broadcasted_iota(jnp.int32, value.shape, value.ndim - 1)
    keep = lane < width - by if by > 0 else lane >= -by
    return jnp.where(keep, rolled, 0.0)


def paint_matrix(paint_weight, paint_bias):
    high = lax.reduce_precision(paint_weight, 8, 7)
    low = lax.reduce_precision(paint_weight - high, 8, 7)
    bias_0 = lax.reduce_precision(paint_bias, 8, 7)
    bias_1 = lax.reduce_precision(paint_bias - bias_0, 8, 7)
    bias_2 = paint_bias - bias_0 - bias_1
    spread = lambda value: jnp.repeat(value, 8, axis=0)
    high, low = spread(high), spread(low)
    shape = (channels * 8, 160)
    row = lax.broadcasted_iota(jnp.int32, shape, 0) % 8
    col = lax.broadcasted_iota(jnp.int32, shape, 1)
    part, in_row = col // 16, col % 16
    total = jnp.zeros(shape, f32)
    for i in range(3):
        for j in range(3):
            here = (in_row == row + 2 * i) & (part % 3 == j) & (part < 9)
            tap = 3 * i + j
            value = jnp.where(part < 6, high[:, tap : tap + 1], low[:, tap : tap + 1])
            total = jnp.where(here, value, total)
    for k, value in enumerate((bias_0, bias_1, bias_2)):
        total = jnp.where(col == 144 + k, spread(value[:, None]), total)
    return total.astype(bf16)


def paint_kernel(edge_ref, mix_ref, x_ref, low_ref, high_ref, w_ref, pool_ref, c_ref, coarse_ref, wide, stack, sums):
    cols = x_ref.shape[-1]
    wide[...] = jnp.zeros_like(wide)
    sums[...] = jnp.zeros_like(sums)
    stack[144:160, :] = jnp.ones((16, cols), bf16)
    first = edge_ref[0] == 0
    last = edge_ref[1] == 0
    row = lax.broadcasted_iota(jnp.int32, (8, 256), 0)
    for p in range(3):
        wide[0, 0:5, :] = low_ref[p]
        wide[0, 5:13, :] = x_ref[p]
        wide[1, 0:7, :] = x_ref[p, 1:8, :]
        wide[1, 7:12, :] = high_ref[p]
        for window in range(2):
            value = wide[window]
            for j in range(3):
                moved = value if j == 1 else shifted(value, 2 * (j - 1))
                upper = moved.astype(bf16)
                lower = (moved - upper.astype(f32)).astype(bf16)
                stack[16 * j : 16 * j + 16, :] = upper
                stack[48 + 16 * j : 64 + 16 * j, :] = lower
                stack[96 + 16 * j : 112 + 16 * j, :] = upper

            def one_chunk(chunk, carry):
                at = pl.ds(pl.multiple_of(chunk * 256, 256), 256)
                before = jnp.dot(w_ref[...], stack[:, at], preferred_element_type=f32)
                total = jnp.zeros((8, 256), f32)
                for c in range(channels):
                    total = total + mix_ref[c] * jnp.tanh(before[8 * c : 8 * c + 8, :])
                if window == 0:
                    total = jnp.where(first & (row < 3), 0.0, total)
                    c_ref[p, 0:8, at] = total
                else:
                    total = jnp.where(last & (row >= 5), 0.0, total)
                    c_ref[p, 8:14, at] = total[2:8]
                return carry

            lax.fori_loop(0, cols // 256, one_chunk, 0, unroll=True)
        value = c_ref[p, 3:11, :]
        sums[p : p + 1, :] = jnp.sum(value[0:4], axis=0, keepdims=True)
        sums[3 + p : 4 + p, :] = jnp.sum(value[4:8], axis=0, keepdims=True)
    c_ref[:, 14:16, :] = jnp.zeros((3, 2, cols), f32)
    quarter = cols // 4
    stacked = jnp.concatenate([sums[:, quarter * v : quarter * (v + 1)] for v in range(4)], axis=0)
    pooled = jnp.dot(stacked, pool_ref[...], precision=highest, preferred_element_type=f32)
    for v in range(4):
        coarse_ref[:, 128 * v : 128 * v + 128] = pooled[8 * v : 8 * v + 8]


def short_kernel_body(k_ref, c_ref, s_ref, held):
    cols = c_ref.shape[-1]
    for p in range(3):
        held[0:16, :] = c_ref[p]
        held[16:24, :] = jnp.zeros((8, cols), f32)
        for window in range(2):
            total = jnp.zeros((8, cols), f32)
            for b in range(5):
                part = jnp.zeros((8, cols), f32)
                for a in range(5):
                    start = 8 * window + a
                    part = part + k_ref[5 * a + b] * held[start : start + 8, :]
                total = total + (part if b == 2 else shifted(part, b - 2))
            s_ref[p, 8 * window : 8 * window + 8, :] = total


def bend_kernel(decay, gain, edge_ref, s_ref, coarse_ref, acc_ref, ec_ref, grow_ref, sent_ref, u_ref, rows, pot, rim):
    cols = s_ref.shape[-1]
    e = decay
    c0, c1 = coarse_ref[0:3, :], coarse_ref[3:6, :]
    up, down = acc_ref[0:3, :], acc_ref[3:6, :]
    rows[12:16, :] = jnp.zeros((4, rows.shape[-1]), f32)
    rows[0:3, :] = e * c0 + e * e * c1 + e * e * down + up * (1.0 / e)
    rows[3:6, :] = c0 + e * c1 + up + e * down
    rows[6:9, :] = c1 + e * c0 + e * up + down
    rows[9:12, :] = e * e * c0 + e * c1 + e * e * up + down * (1.0 / e)
    smooth = gain * jnp.dot(rows[...], ec_ref[...], precision=highest, preferred_element_type=f32)
    stacked = jnp.concatenate([smooth[:, 128 * v : 128 * v + 128] for v in range(4)], axis=0)
    grown = jnp.dot(stacked, grow_ref[...], precision=highest, preferred_element_type=f32)
    long = jnp.concatenate([grown[16 * v : 16 * v + 16] for v in range(4)], axis=1)
    row = lax.broadcasted_iota(jnp.int32, (8, cols), 0)
    lane = lax.broadcasted_iota(jnp.int32, (8, cols), 1) % 128
    top = edge_ref[0] != 0
    bottom = edge_ref[1] != 0
    rim[...] = jnp.zeros_like(rim)
    side = jnp.zeros((8, cols), f32)
    for p in range(3):
        part = s_ref[p]
        wide = jnp.where(
            row < 4,
            jnp.broadcast_to(long[3 + p : 4 + p], (8, cols)),
            jnp.broadcast_to(long[6 + p : 7 + p], (8, cols)),
        )
        here = part[1:9] + wide
        above_row = jnp.where(top, part[0:1] + long[p : p + 1], 0.0)
        below_row = jnp.where(bottom, part[9:10] + long[9 + p : 10 + p], 0.0)
        pot[7:8, :] = above_row
        pot[8:16, :] = here
        pot[16:17, :] = below_row
        rim[p : p + 1, :] = above_row
        rim[3 + p : 4 + p, :] = below_row
        above, below = pot[7:15, :], pot[9:17, :]
        u11 = below - 2.0 * here + above
        u22 = shifted(here, 1) - 2.0 * here + shifted(here, -1)
        step = below - above
        u12 = (shifted(step, 1) - shifted(step, -1)) * 0.25
        side = jnp.where(lane == 2 * p, shifted(here, -1 - 2 * p), side)
        side = jnp.where(lane == 2 * p + 1, shifted(here, 127 - 2 * p), side)
        for d in range(cols // 128):
            at = slice(128 * d, 128 * d + 128)
            sent_ref[5 * d + p] = here[:, at]
            u_ref[9 * d + 3 * p] = u11[:, at]
            u_ref[9 * d + 3 * p + 1] = u12[:, at]
            u_ref[9 * d + 3 * p + 2] = u22[:, at]
    rim_rows = rim[...]
    side = jnp.where(lane == 6, shifted(rim_rows, -7), side)
    side = jnp.where(lane == 7, shifted(rim_rows, 121), side)
    for d in range(cols // 128):
        at = slice(128 * d, 128 * d + 128)
        sent_ref[5 * d + 3] = rim_rows[:, at]
        sent_ref[5 * d + 4] = side[:, at]


def advance(previous, current, u11, u12, u22, mixing, bending):
    kept = 1.0 - mixing
    bent = (
        u11 * current[0] + u12 * current[2],
        u11 * current[1] + u12 * current[3],
        u12 * current[0] + u22 * current[2],
        u12 * current[1] + u22 * current[3],
    )
    return tuple(kept * previous[i] + mixing * current[i] - bending * bent[i] for i in range(4))


def beside(value, left, right):
    lane = lax.broadcasted_iota(jnp.int32, value.shape, 1)
    before = jnp.where(lane == 0, jnp.broadcast_to(left, value.shape), pltpu.roll(value, 1, 1))
    after = jnp.where(lane == 127, jnp.broadcast_to(right, value.shape), pltpu.roll(value, 127, 1))
    return before, after


def over_rows(value, above, below):
    row = lax.broadcasted_iota(jnp.int32, value.shape, 0)
    before = jnp.where(row == 0, jnp.broadcast_to(above, value.shape), pltpu.roll(value, 1, 0))
    after = jnp.where(row == 7, jnp.broadcast_to(below, value.shape), pltpu.roll(value, 7, 0))
    return before, after


def scan_kernel(mixing_ref, bending_ref, sent_ref, state_ref):
    one = jnp.ones((8, 128), f32)
    zero = jnp.zeros((8, 128), f32)
    groups = sent_ref.shape[0] // 5

    def one_group(g, carry):
        previous, current = carry
        for i in range(4):
            state_ref[8 * g + i] = previous[i]
            state_ref[8 * g + 4 + i] = current[i]
        rim = sent_ref[5 * g + 3]
        side = sent_ref[5 * g + 4]
        rim_left, rim_right = beside(rim, side[:, 6:7], side[:, 7:8])
        rim_step = rim_right - rim_left
        for p in range(3):
            k = 3 * g + p
            here = sent_ref[5 * g + p]
            above, below = over_rows(here, rim[p : p + 1], rim[3 + p : 4 + p])
            left, right = beside(here, side[:, 2 * p : 2 * p + 1], side[:, 2 * p + 1 : 2 * p + 2])
            u11 = below - 2.0 * here + above
            u22 = right - 2.0 * here + left
            step_above, step_below = over_rows(right - left, rim_step[p : p + 1], rim_step[3 + p : 4 + p])
            u12 = (step_below - step_above) * 0.25
            later = advance(previous, current, u11, u12, u22, mixing_ref[k], bending_ref[k])
            previous, current = current, later
        return (previous, current)

    start = (one, zero, zero, one)
    lax.fori_loop(0, groups, one_group, (start, start), unroll=True)


def final_kernel(mixing_ref, bending_ref, u_ref, state_ref, out_ref):
    blocks = u_ref.shape[0] // 9

    def one_block(d, carry):
        at = pl.ds(pl.multiple_of(d * 128, 128), 128)
        previous = tuple(state_ref[8 * d + i] for i in range(4))
        current = tuple(state_ref[8 * d + 4 + i] for i in range(4))
        for p in range(3):
            k = 9 * d + 3 * p
            later = advance(
                previous, current, u_ref[k], u_ref[k + 1], u_ref[k + 2], mixing_ref[p], bending_ref[p]
            )
            for i in range(4):
                out_ref[i, p, :, at] = later[i]
            previous, current = current, later
        return carry

    lax.fori_loop(0, blocks, one_block, 0)


vmem = pl.BlockSpec(memory_space=pltpu.VMEM)
smem = pl.BlockSpec(memory_space=pltpu.SMEM)


def sds(*shape):
    return jax.ShapeDtypeStruct(shape, f32)


def call(kernel, name, n_smem, n_vmem, out_shape, scratch=(), cost=(0, 0, 0)):
    outs = jax.tree.map(lambda _: vmem, out_shape)
    return pl.pallas_call(
        kernel,
        name=name,
        out_shape=out_shape,
        in_specs=[smem] * n_smem + [vmem] * n_vmem,
        out_specs=outs,
        scratch_shapes=list(scratch),
        cost_estimate=pl.CostEstimate(flops=cost[0], bytes_accessed=cost[1], transcendentals=cost[2]),
        compiler_params=pltpu.CompilerParams(vmem_limit_bytes=24 << 20),
    )


def row_scan(message, near_index, far_index):
    rows, cols = message.shape
    near, far = lax.axis_size("near"), lax.axis_size("far")
    forward = lax.broadcasted_iota(jnp.int32, (1, rows, 1), 1) < 3
    decayed = lambda tiles: jnp.exp(tiles.astype(f32) / -8.0)

    def everyone(value, axis, count):
        copies = jnp.broadcast_to(value[None], (count, rows, cols))
        return lax.all_to_all(copies, axis, 0, 0, tiled=True)

    q = lax.broadcasted_iota(jnp.int32, (near, 1, 1), 0)
    gap = jnp.where(forward, near_index - q, q - near_index) - 1
    to_edge = jnp.where(forward, near - 1 - q, q)
    received = everyone(message, "near", near)
    total = jnp.sum(jnp.where(gap >= 0, decayed(jnp.maximum(gap, 0)), 0.0) * received, axis=0)
    run = jnp.sum(decayed(to_edge) * received, axis=0)

    w = lax.broadcasted_iota(jnp.int32, (far, 1, 1), 0)
    runs = jnp.where(forward, far_index - w, w - far_index) - 1
    inside = jnp.where(forward, near_index, near - 1 - near_index)
    weight = jnp.where(runs >= 0, decayed(jnp.maximum(runs, 0) * near + inside), 0.0)
    return total + jnp.sum(weight * everyone(run, "far", far), axis=0)


def body(density, plane_slot, paint_weight, paint_bias, mix_weight, short_kernel):
    plane_count, row_count, col_count = density.shape
    tile = ("far", "near")
    near_index, far_index = lax.axis_index("near"), lax.axis_index("far")
    tile_count = lax.axis_size("far") * lax.axis_size("near")
    group_count = lax.axis_size("plane")
    tile_index = far_index * lax.axis_size("near") + near_index
    plane_index = lax.axis_index("plane")
    coarse_cols = col_count // 4
    row_scale = row_count * tile_count / 16.0
    col_scale = col_count / 16.0
    long_gain = 1.0 / math.sqrt(row_scale * col_scale)
    decay = math.exp(-1.0 / row_scale)

    up = [(i, i + 1) for i in range(tile_count - 1)]
    low = lax.ppermute(density[:, 3:8, :], tile, up)
    high = lax.ppermute(density[:, 0:5, :], tile, [(b, a) for a, b in up])

    edge = jnp.stack([tile_index, tile_count - 1 - tile_index]).astype(jnp.int32)
    mixing, bending = distances(plane_slot, 2 * plane_slot.shape[0])
    mixing_here = lax.dynamic_slice_in_dim(mixing, plane_index * plane_count, plane_count)
    bending_here = lax.dynamic_slice_in_dim(bending, plane_index * plane_count, plane_count)
    weights = paint_matrix(paint_weight, paint_bias)
    gap = lax.broadcasted_iota(jnp.int32, (coarse_cols, coarse_cols), 0) - lax.broadcasted_iota(
        jnp.int32, (coarse_cols, coarse_cols), 1
    )
    col_kernel = jnp.exp(-jnp.abs(gap.astype(f32)) / col_scale)
    pool = jnp.where(
        lax.broadcasted_iota(jnp.int32, (512, 128), 0) // 4 == lax.broadcasted_iota(jnp.int32, (512, 128), 1),
        1.0 / 16.0,
        0.0,
    ).astype(f32)
    grow = jnp.where(
        lax.broadcasted_iota(jnp.int32, (128, 512), 1) // 4 == lax.broadcasted_iota(jnp.int32, (128, 512), 0), 1.0, 0.0
    ).astype(f32)

    convergence, coarse = call(
        paint_kernel,
        "paint",
        2,
        5,
        (sds(3, 16, col_count), sds(8, coarse_cols)),
        [pltpu.VMEM((2, 16, col_count), f32), pltpu.VMEM((160, col_count), bf16), pltpu.VMEM((8, col_count), f32)],
        (8 * 10**9, 2 * 10**6, 10**6),
    )(edge, mix_weight, density, low, high, weights, pool)
    coarse, convergence, mixing, bending, mixing_here, bending_here = lax.optimization_barrier(
        (coarse, convergence, mixing, bending, mixing_here, bending_here)
    )

    e = decay
    c0, c1 = coarse[0:3], coarse[3:6]
    message = jnp.concatenate([e * e * c0 + e * c1, e * c0 + e * e * c1, jnp.zeros_like(coarse[0:2])], axis=0)
    received = row_scan(message, near_index, far_index)

    short_part = call(
        short_kernel_body,
        "short",
        1,
        1,
        sds(3, 16, col_count),
        [pltpu.VMEM((24, col_count), f32)],
        (10**7, 10**6, 0),
    )(short_kernel.reshape(25), convergence)

    sent, shear = call(
        functools.partial(bend_kernel, decay, long_gain),
        "bend",
        1,
        5,
        (sds(group_count * 5, 8, 128), sds(group_count * 9, 8, 128)),
        [pltpu.VMEM((16, coarse_cols), f32), pltpu.VMEM((24, col_count), f32), pltpu.VMEM((8, col_count), f32)],
        (10**8, 2 * 10**6, 0),
    )(edge, short_part, coarse, received, col_kernel, grow)

    gathered = lax.all_to_all(sent, "plane", 0, 0, tiled=True)
    states = call(scan_kernel, "scan", 2, 1, sds(group_count * 8, 8, 128), (), (10**7, 10**6, 0))(
        mixing, bending, gathered
    )
    mine = lax.all_to_all(states, "plane", 0, 0, tiled=True)
    return call(final_kernel, "final", 2, 2, sds(4, plane_count, row_count, col_count), (), (10**7, 10**6, 0))(
        mixing_here, bending_here, shear, mine
    )


def solution(mesh):
    planes, tiles = mesh.devices.shape
    split = Mesh(mesh.devices.reshape(planes, 4, tiles // 4), ("plane", "far", "near"))
    tile = ("far", "near")
    placed = (P("plane", tile, None), P(), P(), P(), P(), P())
    return jax.shard_map(
        body, mesh=split, in_specs=placed, out_specs=P(None, "plane", tile, None), check_vma=False
    )
```

```python
import functools
import math

import jax
import jax.numpy as jnp
from jax import lax
from jax.experimental import pallas as pl
from jax.experimental.pallas import tpu as pltpu
from jax.sharding import Mesh
from jax.sharding import PartitionSpec as P

f32 = jnp.float32
bf16 = jnp.bfloat16
lens_gain = 0.25
channels = 32
highest = lax.Precision.HIGHEST


def distances(plane_slot, slot_total):
    distance = (plane_slot.astype(f32) + 1.0) / slot_total
    before = jnp.concatenate([jnp.zeros((1,), f32), distance[:-1]])
    after = jnp.concatenate([distance[1:], jnp.full((1,), (slot_total + 1.0) / slot_total, f32)])
    mixing = before * (after - distance) / (distance * (after - before))
    bending = lens_gain * (after - distance) / after
    return (mixing, bending)


def shifted(value, by):
    width = value.shape[-1]
    rolled = pltpu.roll(value, (-by) % width, value.ndim - 1)
    lane = lax.broadcasted_iota(jnp.int32, value.shape, value.ndim - 1)
    keep = lane < width - by if by > 0 else lane >= -by
    return jnp.where(keep, rolled, 0.0)


def tile_place():
    near, far = lax.axis_index("near"), lax.axis_index("far")
    return near, far, far * lax.axis_size("near") + near


def weights_kernel(w_ref, b_ref, out_ref, pool_ref):
    group = lax.broadcasted_iota(jnp.int32, pool_ref.shape, 0) // 4
    pool_ref[...] = jnp.where(group == lax.broadcasted_iota(jnp.int32, pool_ref.shape, 1), 1.0 / 16.0, 0.0)
    shape = (8, 160)
    row = lax.broadcasted_iota(jnp.int32, shape, 0)
    col = lax.broadcasted_iota(jnp.int32, shape, 1)
    part, in_row = col // 16, col % 16
    taps = []
    for i in range(3):
        for j in range(3):
            here = (in_row == row + 2 * i) & (part % 3 == j) & (part < 9)
            taps.append(jnp.where(here, 1.0, 0.0))
    bias_here = jnp.where((col >= 144) & (col < 147), 1.0, 0.0)
    for c in range(channels):
        exact = b_ref[c] * bias_here
        for t in range(9):
            exact = exact + w_ref[c, t] * taps[t]
        first = exact.astype(bf16).astype(f32)
        second = (exact - first).astype(bf16).astype(f32)
        third = exact - first - second
        value = jnp.where((col < 96) | (col == 144), first, jnp.where(col < 146, second, third))
        out_ref[8 * c : 8 * c + 8, :] = value.astype(bf16)


def paint_window(w_ref, mix_ref, stack, value, store):
    cols = value.shape[-1]
    for j in range(3):
        moved = value if j == 1 else shifted(value, 2 * (j - 1))
        upper = moved.astype(bf16)
        lower = (moved - upper.astype(f32)).astype(bf16)
        stack[16 * j : 16 * j + 16, :] = upper
        stack[48 + 16 * j : 64 + 16 * j, :] = lower
        stack[96 + 16 * j : 112 + 16 * j, :] = upper

    def one_chunk(chunk, carry):
        at = pl.ds(pl.multiple_of(chunk * 256, 256), 256)
        before = jnp.dot(w_ref[...], stack[:, at], preferred_element_type=f32)
        total = jnp.zeros((8, 256), f32)
        for c in range(channels):
            total = total + mix_ref[channels + c] * jnp.tanh(before[8 * c : 8 * c + 8, :])
        store(at, total)
        return carry

    lax.fori_loop(0, cols // 256, one_chunk, 0, unroll=True)


def paint_kernel(decay, mix_ref, x_ref, low_ref, high_ref, w_ref, pool_ref, c_ref, coarse_ref, copies_ref, wide, stack, sums):
    cols = x_ref.shape[-1]
    wide[12:16, :] = jnp.zeros((4, cols), f32)
    sums[6:8, :] = jnp.zeros((2, cols), f32)
    stack[144:160, :] = jnp.ones((16, cols), bf16)
    for p in range(3):
        wide[0:2, :] = low_ref[p, 3:5, :]
        wide[2:10, :] = x_ref[p]
        wide[10:12, :] = high_ref[p, 0:2, :]

        def store(at, total):
            c_ref[p, :, at] = total
            sums[p : p + 1, at] = jnp.sum(total[0:4], axis=0, keepdims=True)
            sums[3 + p : 4 + p, at] = jnp.sum(total[4:8], axis=0, keepdims=True)

        paint_window(w_ref, mix_ref, stack, wide[...], store)
    quarter = cols // 4
    stacked = jnp.concatenate([sums[:, quarter * v : quarter * (v + 1)] for v in range(4)], axis=0)
    pooled = jnp.dot(stacked, pool_ref[...], precision=highest, preferred_element_type=f32)
    e = decay
    row = lax.broadcasted_iota(jnp.int32, (8, 128), 0)
    for v in range(4):
        at = slice(128 * v, 128 * v + 128)
        here = pooled[8 * v : 8 * v + 8]
        coarse_ref[:, at] = here
        turned = jnp.where(row < 3, pltpu.roll(here, 5, 0), pltpu.roll(here, 3, 0))
        upper = jnp.where(row < 3, here, turned)
        lower = jnp.where(row < 3, turned, here)
        message = jnp.where(row < 3, e * e * upper + e * lower, e * upper + e * e * lower)
        message = jnp.where(row < 6, message, 0.0)
        for q in range(copies_ref.shape[0] // 8):
            copies_ref[8 * q : 8 * q + 8, at] = message


def edge_kernel(mix_ref, x_ref, low_ref, high_ref, w_ref, main_ref, c_ref, wide, stack):
    cols = x_ref.shape[-1]
    near, far, tile = tile_place()
    top = tile != 0
    bottom = tile != lax.axis_size("near") * lax.axis_size("far") - 1
    stack[144:160, :] = jnp.ones((16, cols), bf16)
    c_ref[:, 14:16, :] = jnp.zeros((3, 2, cols), f32)
    for p in range(3):
        wide[0:5, :] = low_ref[p]
        wide[5:13, :] = x_ref[p]
        wide[13:16, :] = jnp.zeros((3, cols), f32)

        def store_above(at, total):
            c_ref[p, 0:3, at] = jnp.where(top, total[0:3], 0.0)

        paint_window(w_ref, mix_ref, stack, wide[...], store_above)
        wide[0:7, :] = x_ref[p, 1:8, :]
        wide[7:12, :] = high_ref[p]
        wide[12:16, :] = jnp.zeros((4, cols), f32)

        def store_below(at, total):
            c_ref[p, 11:14, at] = jnp.where(bottom, total[5:8], 0.0)

        paint_window(w_ref, mix_ref, stack, wide[...], store_below)
        c_ref[p, 3:11, :] = main_ref[p]


def tile_decay(tiles, used):
    return jnp.where(used, jnp.exp(jnp.maximum(tiles, 0).astype(f32) / -8.0), 0.0)


def runs_kernel(received_ref, total_ref, copies_ref):
    near = lax.axis_index("near")
    count = received_ref.shape[0] // 8
    cols = received_ref.shape[-1]
    forward = lax.broadcasted_iota(jnp.int32, (8, 128), 0) < 3
    totals = [jnp.zeros((8, 128), f32)] * (cols // 128)
    runs = [jnp.zeros((8, 128), f32)] * (cols // 128)
    for q in range(count):
        gap = jnp.where(forward, near - q, q - near) - 1
        weight = tile_decay(gap, gap >= 0)
        to_edge = jnp.where(forward, math.exp(-(count - 1 - q) / 8.0), math.exp(-q / 8.0))
        for v in range(cols // 128):
            value = received_ref[8 * q : 8 * q + 8, 128 * v : 128 * v + 128]
            totals[v] = totals[v] + weight * value
            runs[v] = runs[v] + to_edge * value
    for v in range(cols // 128):
        at = slice(128 * v, 128 * v + 128)
        total_ref[:, at] = totals[v]
        for w in range(copies_ref.shape[0] // 8):
            copies_ref[8 * w : 8 * w + 8, at] = runs[v]


def short_kernel_body(scale, k_ref, c_ref, s_ref, ec_ref, held):
    cols = c_ref.shape[-1]
    for p in range(3):
        held[0:16, :] = c_ref[p]
        held[16:24, :] = jnp.zeros((8, cols), f32)
        for window in range(2):
            total = jnp.zeros((8, cols), f32)
            for b in range(5):
                part = jnp.zeros((8, cols), f32)
                for a in range(5):
                    start = 8 * window + a
                    part = part + k_ref[a, b] * held[start : start + 8, :]
                total = total + (part if b == 2 else shifted(part, b - 2))
            s_ref[p, 8 * window : 8 * window + 8, :] = total
    gap = lax.broadcasted_iota(jnp.int32, ec_ref.shape, 0) - lax.broadcasted_iota(jnp.int32, ec_ref.shape, 1)
    ec_ref[...] = jnp.exp(-jnp.abs(gap.astype(f32)) / scale)


def side_matrix(back):
    shape = (128, 128)
    i = lax.broadcasted_iota(jnp.int32, shape, 1 if back else 0)
    j = lax.broadcasted_iota(jnp.int32, shape, 0 if back else 1)
    return jnp.where(j // 8 == i, jnp.where(i < 8, 1.0, 0.0), 0.0)


def own_lane():
    shape = (8, 128)
    lane = lax.broadcasted_iota(jnp.int32, shape, 1)
    return (lane < 64) & (lane % 8 == lax.broadcasted_iota(jnp.int32, shape, 0))


def bend_kernel(decay, gain, s_ref, coarse_ref, total_ref, run_ref, ec_ref, sent_ref, pot_ref, rows, rim):
    cols = s_ref.shape[-1]
    e = decay
    near, far, tile = tile_place()
    near_count = lax.axis_size("near")
    forward = lax.broadcasted_iota(jnp.int32, (8, rows.shape[-1]), 0) < 3
    acc = total_ref[...]
    inside = jnp.where(forward, near, near_count - 1 - near)
    for w in range(run_ref.shape[0] // 8):
        gap = jnp.where(forward, far - w, w - far) - 1
        acc = acc + tile_decay(gap * near_count + inside, gap >= 0) * run_ref[8 * w : 8 * w + 8, :]
    c0, c1 = coarse_ref[0:3, :], coarse_ref[3:6, :]
    up, down = acc[0:3, :], acc[3:6, :]
    rows[12:16, :] = jnp.zeros((4, rows.shape[-1]), f32)
    rows[0:3, :] = e * c0 + e * e * c1 + e * e * down + up * (1.0 / e)
    rows[3:6, :] = c0 + e * c1 + up + e * down
    rows[6:9, :] = c1 + e * c0 + e * up + down
    rows[9:12, :] = e * e * c0 + e * c1 + e * e * up + down * (1.0 / e)
    smooth = gain * jnp.dot(rows[...], ec_ref[...], precision=highest, preferred_element_type=f32)
    stacked = jnp.concatenate([smooth[:, 128 * v : 128 * v + 128] for v in range(4)], axis=0)
    shape = (128, 512)
    group = lax.broadcasted_iota(jnp.int32, shape, 1) // 4
    grow = jnp.where(group == lax.broadcasted_iota(jnp.int32, shape, 0), 1.0, 0.0)
    grown = jnp.dot(stacked, grow, precision=highest, preferred_element_type=f32)
    long = jnp.concatenate([grown[16 * v : 16 * v + 16] for v in range(4)], axis=1)
    row = lax.broadcasted_iota(jnp.int32, (8, cols), 0)
    lane = lax.broadcasted_iota(jnp.int32, (8, cols), 1) % 128
    top = tile != 0
    bottom = tile != near_count * lax.axis_size("far") - 1
    rim[6:8, :] = jnp.zeros((2, cols), f32)
    side = jnp.zeros((8, cols), f32)
    for p in range(3):
        part = s_ref[p]
        wide = jnp.where(
            row < 4,
            jnp.broadcast_to(long[3 + p : 4 + p], (8, cols)),
            jnp.broadcast_to(long[6 + p : 7 + p], (8, cols)),
        )
        here = part[1:9] + wide
        above_row = jnp.where(top, part[0:1] + long[p : p + 1], 0.0)
        below_row = jnp.where(bottom, part[9:10] + long[9 + p : 10 + p], 0.0)
        pot_ref[p, 7:8, :] = above_row
        pot_ref[p, 8:16, :] = here
        pot_ref[p, 16:17, :] = below_row
        rim[p : p + 1, :] = above_row
        rim[3 + p : 4 + p, :] = below_row
        side = jnp.where(lane == 2 * p, shifted(here, -1 - 2 * p), side)
        side = jnp.where(lane == 2 * p + 1, shifted(here, 127 - 2 * p), side)
        for d in range(cols // 128):
            at = slice(128 * d, 128 * d + 128)
            sent_ref[4 * d + p] = here[:, at]
    rim_rows = rim[...]
    side = jnp.where(lane == 6, shifted(rim_rows, -7), side)
    side = jnp.where(lane == 7, shifted(rim_rows, 121), side)
    blocks = cols // 128
    spread = side_matrix(False)
    lined = jnp.concatenate([side[:, 128 * d : 128 * d + 128] for d in range(blocks)], axis=0)
    lined = jnp.dot(lined, spread, precision=highest, preferred_element_type=f32)
    own = own_lane()
    row = lax.broadcasted_iota(jnp.int32, (8, 128), 0)
    for d in range(blocks):
        line = jnp.sum(jnp.where(own, lined[8 * d : 8 * d + 8], 0.0), axis=0, keepdims=True)
        line = jnp.broadcast_to(line, (8, 128))
        sent_ref[4 * d + 3] = jnp.where(row == 6, line, rim_rows[:, 128 * d : 128 * d + 128])


def own_hessian(pot_ref, u_ref):
    cols = pot_ref.shape[-1]
    for p in range(3):
        here = pot_ref[p, 8:16, :]
        above, below = pot_ref[p, 7:15, :], pot_ref[p, 9:17, :]
        u11 = below - 2.0 * here + above
        u22 = shifted(here, 1) - 2.0 * here + shifted(here, -1)
        step = below - above
        u12 = (shifted(step, 1) - shifted(step, -1)) * 0.25
        for d in range(cols // 128):
            at = slice(128 * d, 128 * d + 128)
            u_ref[9 * d + 3 * p] = u11[:, at]
            u_ref[9 * d + 3 * p + 1] = u12[:, at]
            u_ref[9 * d + 3 * p + 2] = u22[:, at]


def advance(previous, current, u11, u12, u22, mixing, bending):
    kept = 1.0 - mixing
    bent = (
        u11 * current[0] + u12 * current[2],
        u11 * current[1] + u12 * current[3],
        u12 * current[0] + u22 * current[2],
        u12 * current[1] + u22 * current[3],
    )
    return tuple(kept * previous[i] + mixing * current[i] - bending * bent[i] for i in range(4))


def beside(value, left, right):
    lane = lax.broadcasted_iota(jnp.int32, value.shape, 1)
    before = jnp.where(lane == 0, jnp.broadcast_to(left, value.shape), pltpu.roll(value, 1, 1))
    after = jnp.where(lane == 127, jnp.broadcast_to(right, value.shape), pltpu.roll(value, 127, 1))
    return before, after


def over_rows(value, above, below):
    row = lax.broadcasted_iota(jnp.int32, value.shape, 0)
    before = jnp.where(row == 0, jnp.broadcast_to(above, value.shape), pltpu.roll(value, 1, 0))
    after = jnp.where(row == 7, jnp.broadcast_to(below, value.shape), pltpu.roll(value, 7, 0))
    return before, after


def scan_kernel(mixing_ref, bending_ref, sent_ref, pot_ref, state_ref, u_ref):
    own_hessian(pot_ref, u_ref)
    one = jnp.ones((8, 128), f32)
    zero = jnp.zeros((8, 128), f32)
    groups = sent_ref.shape[0] // 4
    own = own_lane()
    lines = [jnp.broadcast_to(sent_ref[4 * g + 3, 6:7, :], (8, 128)) for g in range(groups)]
    lined = jnp.concatenate([jnp.where(own, line, 0.0) for line in lines], axis=0)
    sides = jnp.dot(lined, side_matrix(True), precision=highest, preferred_element_type=f32)

    previous = current = (one, zero, zero, one)
    for g in range(groups):
        for i in range(4):
            state_ref[8 * g + i] = previous[i]
            state_ref[8 * g + 4 + i] = current[i]
        rim = sent_ref[4 * g + 3]
        side = sides[8 * g : 8 * g + 8]
        rim_left, rim_right = beside(rim, side[:, 6:7], side[:, 7:8])
        rim_step = rim_right - rim_left
        for p in range(3):
            k = 3 * g + p
            here = sent_ref[4 * g + p]
            above, below = over_rows(here, rim[p : p + 1], rim[3 + p : 4 + p])
            left, right = beside(here, side[:, 2 * p : 2 * p + 1], side[:, 2 * p + 1 : 2 * p + 2])
            u11 = below - 2.0 * here + above
            u22 = right - 2.0 * here + left
            step_above, step_below = over_rows(right - left, rim_step[p : p + 1], rim_step[3 + p : 4 + p])
            u12 = (step_below - step_above) * 0.25
            later = advance(previous, current, u11, u12, u22, mixing_ref[k], bending_ref[k])
            previous, current = current, later


def final_kernel(mixing_ref, bending_ref, u_ref, state_ref, out_ref):
    blocks = u_ref.shape[0] // 9
    first = 3 * lax.axis_index("plane")

    def one_block(d, carry):
        at = pl.ds(pl.multiple_of(d * 128, 128), 128)
        previous = tuple(state_ref[8 * d + i] for i in range(4))
        current = tuple(state_ref[8 * d + 4 + i] for i in range(4))
        for p in range(3):
            k = 9 * d + 3 * p
            later = advance(
                previous,
                current,
                u_ref[k],
                u_ref[k + 1],
                u_ref[k + 2],
                mixing_ref[first + p],
                bending_ref[first + p],
            )
            for i in range(4):
                out_ref[i, p, :, at] = later[i]
            previous, current = current, later
        return carry

    lax.fori_loop(0, blocks, one_block, 0, unroll=True)


vmem = pl.BlockSpec(memory_space=pltpu.VMEM)
smem = pl.BlockSpec(memory_space=pltpu.SMEM)


def sds(*shape):
    return jax.ShapeDtypeStruct(shape, f32)


def call(kernel, name, n_smem, n_vmem, out_shape, scratch=(), cost=(0, 0, 0)):
    outs = jax.tree.map(lambda _: vmem, out_shape)
    return pl.pallas_call(
        kernel,
        name=name,
        out_shape=out_shape,
        in_specs=[smem] * n_smem + [vmem] * n_vmem,
        out_specs=outs,
        scratch_shapes=list(scratch),
        cost_estimate=pl.CostEstimate(flops=cost[0], bytes_accessed=cost[1], transcendentals=cost[2]),
        compiler_params=pltpu.CompilerParams(vmem_limit_bytes=24 << 20),
    )


def body(density, plane_slot, paint_weight, paint_bias, mix_weight, short_kernel):
    plane_count, row_count, col_count = density.shape
    tile = ("far", "near")
    near_count, far_count = lax.axis_size("near"), lax.axis_size("far")
    tile_count = far_count * near_count
    group_count = lax.axis_size("plane")
    coarse_cols = col_count // 4
    row_scale = row_count * tile_count / 16.0
    col_scale = col_count / 16.0
    long_gain = 1.0 / math.sqrt(row_scale * col_scale)
    decay = math.exp(-1.0 / row_scale)

    up = [(i, i + 1) for i in range(tile_count - 1)]
    low = lax.ppermute(density[:, 3:8, :], tile, up)
    high = lax.ppermute(density[:, 0:5, :], tile, [(b, a) for a, b in up])

    scalars = jnp.concatenate([paint_bias, mix_weight])
    weights, pool = call(
        weights_kernel,
        "weights",
        2,
        0,
        (jax.ShapeDtypeStruct((channels * 8, 160), bf16), sds(col_count // 4, col_count // 16)),
        (),
        (10**6, 10**5, 0),
    )(paint_weight, scalars)
    mixing, bending = distances(plane_slot, 2 * plane_slot.shape[0])
    main, coarse, copies = call(
        functools.partial(paint_kernel, decay),
        "paint",
        1,
        5,
        (
            sds(plane_count, row_count, col_count),
            sds(8, coarse_cols),
            sds(8 * near_count, coarse_cols),
        ),
        [pltpu.VMEM((16, col_count), f32), pltpu.VMEM((160, col_count), bf16), pltpu.VMEM((8, col_count), f32)],
        (4 * 10**9, 2 * 10**6, 10**6),
    )(scalars, density, low, high, weights, pool)
    copies, mixing, bending = lax.optimization_barrier((copies, mixing, bending))

    received = lax.all_to_all(copies, "near", 0, 0, tiled=True)
    convergence = call(
        edge_kernel,
        "edges",
        1,
        5,
        sds(plane_count, 16, col_count),
        [pltpu.VMEM((16, col_count), f32), pltpu.VMEM((160, col_count), bf16)],
        (8 * 10**9, 2 * 10**6, 10**6),
    )(scalars, density, low, high, weights, main)
    total, run_copies = call(
        runs_kernel, "runs", 0, 1, (sds(8, coarse_cols), sds(8 * far_count, coarse_cols)), (), (10**6, 10**5, 0)
    )(received)
    convergence, run_copies = lax.optimization_barrier((convergence, run_copies))
    runs = lax.all_to_all(run_copies, "far", 0, 0, tiled=True)
    short_part, col_kernel = call(
        functools.partial(short_kernel_body, col_scale),
        "short",
        1,
        1,
        (sds(plane_count, 16, col_count), sds(coarse_cols, coarse_cols)),
        [pltpu.VMEM((24, col_count), f32)],
        (10**7, 10**6, 0),
    )(short_kernel, convergence)

    sent, potential = call(
        functools.partial(bend_kernel, decay, long_gain),
        "bend",
        0,
        5,
        (sds(group_count * 4, 8, 128), sds(plane_count, 24, col_count)),
        [pltpu.VMEM((16, coarse_cols), f32), pltpu.VMEM((8, col_count), f32)],
        (10**8, 2 * 10**6, 0),
    )(short_part, coarse, total, runs, col_kernel)

    gathered = lax.all_to_all(sent, "plane", 0, 0, tiled=True)
    states, shear = call(
        scan_kernel,
        "scan",
        2,
        2,
        (sds(group_count * 8, 8, 128), sds(group_count * 9, 8, 128)),
        (),
        (10**7, 10**6, 0),
    )(mixing, bending, gathered, potential)
    mine = lax.all_to_all(states, "plane", 0, 0, tiled=True)
    return call(final_kernel, "final", 2, 2, sds(4, plane_count, row_count, col_count), (), (10**7, 10**6, 0))(
        mixing, bending, shear, mine
    )


def solution(mesh):
    planes, tiles = mesh.devices.shape
    split = Mesh(mesh.devices.reshape(planes, 4, tiles // 4), ("plane", "far", "near"))
    tile = ("far", "near")
    placed = (P("plane", tile, None), P(), P(), P(), P(), P())
    return jax.shard_map(
        body, mesh=split, in_specs=placed, out_specs=P(None, "plane", tile, None), check_vma=False
    )
```

```python
import functools
import math

import jax
import jax.numpy as jnp
from jax import lax
from jax.experimental import pallas as pl
from jax.experimental.pallas import tpu as pltpu
from jax.sharding import Mesh
from jax.sharding import PartitionSpec as P

f32 = jnp.float32
bf16 = jnp.bfloat16
lens_gain = 0.25
channels = 32
highest = lax.Precision.HIGHEST


def distances(plane_slot, slot_total):
    distance = (plane_slot.astype(f32) + 1.0) / slot_total
    before = jnp.concatenate([jnp.zeros((1,), f32), distance[:-1]])
    after = jnp.concatenate([distance[1:], jnp.full((1,), (slot_total + 1.0) / slot_total, f32)])
    mixing = before * (after - distance) / (distance * (after - before))
    bending = lens_gain * (after - distance) / after
    return (mixing, bending)


def shifted(value, by):
    width = value.shape[-1]
    rolled = pltpu.roll(value, (-by) % width, value.ndim - 1)
    lane = lax.broadcasted_iota(jnp.int32, value.shape, value.ndim - 1)
    keep = lane < width - by if by > 0 else lane >= -by
    return jnp.where(keep, rolled, 0.0)


def tile_place():
    near, far = lax.axis_index("near"), lax.axis_index("far")
    return near, far, far * lax.axis_size("near") + near


def weights_kernel(w_ref, b_ref, out_ref, pool_ref):
    group = lax.broadcasted_iota(jnp.int32, pool_ref.shape, 0) // 4
    pool_ref[...] = jnp.where(group == lax.broadcasted_iota(jnp.int32, pool_ref.shape, 1), 1.0 / 16.0, 0.0)
    shape = (8, 160)
    row = lax.broadcasted_iota(jnp.int32, shape, 0)
    col = lax.broadcasted_iota(jnp.int32, shape, 1)
    part, in_row = col // 16, col % 16
    taps = []
    for i in range(3):
        for j in range(3):
            here = (in_row == row + 2 * i) & (part % 3 == j) & (part < 9)
            taps.append(jnp.where(here, 1.0, 0.0))
    bias_here = jnp.where((col >= 144) & (col < 147), 1.0, 0.0)
    for c in range(channels):
        exact = b_ref[c] * bias_here
        for t in range(9):
            exact = exact + w_ref[c, t] * taps[t]
        first = exact.astype(bf16).astype(f32)
        second = (exact - first).astype(bf16).astype(f32)
        third = exact - first - second
        value = jnp.where((col < 96) | (col == 144), first, jnp.where(col < 146, second, third))
        out_ref[8 * c : 8 * c + 8, :] = value.astype(bf16)


def paint_window(w_ref, mix_ref, stack, value, store):
    cols = value.shape[-1]
    for j in range(3):
        moved = value if j == 1 else shifted(value, 2 * (j - 1))
        upper = moved.astype(bf16)
        lower = (moved - upper.astype(f32)).astype(bf16)
        stack[16 * j : 16 * j + 16, :] = upper
        stack[48 + 16 * j : 64 + 16 * j, :] = lower
        stack[96 + 16 * j : 112 + 16 * j, :] = upper

    def one_chunk(chunk, carry):
        at = pl.ds(pl.multiple_of(chunk * 256, 256), 256)
        before = jnp.dot(w_ref[...], stack[:, at], preferred_element_type=f32)
        total = jnp.zeros((8, 256), f32)
        for c in range(channels):
            total = total + mix_ref[channels + c] * jnp.tanh(before[8 * c : 8 * c + 8, :])
        store(at, total)
        return carry

    lax.fori_loop(0, cols // 256, one_chunk, 0, unroll=True)


def paint_kernel(decay, mix_ref, x_ref, low_ref, high_ref, w_ref, pool_ref, c_ref, coarse_ref, copies_ref, wide, stack, sums):
    cols = x_ref.shape[-1]
    wide[12:16, :] = jnp.zeros((4, cols), f32)
    sums[6:8, :] = jnp.zeros((2, cols), f32)
    stack[144:160, :] = jnp.ones((16, cols), bf16)
    for p in range(3):
        wide[0:2, :] = low_ref[p, 3:5, :]
        wide[2:10, :] = x_ref[p]
        wide[10:12, :] = high_ref[p, 0:2, :]

        def store(at, total):
            c_ref[p, :, at] = total
            sums[p : p + 1, at] = jnp.sum(total[0:4], axis=0, keepdims=True)
            sums[3 + p : 4 + p, at] = jnp.sum(total[4:8], axis=0, keepdims=True)

        paint_window(w_ref, mix_ref, stack, wide[...], store)
    quarter = cols // 4
    stacked = jnp.concatenate([sums[:, quarter * v : quarter * (v + 1)] for v in range(4)], axis=0)
    pooled = jnp.dot(stacked, pool_ref[...], precision=highest, preferred_element_type=f32)
    e = decay
    row = lax.broadcasted_iota(jnp.int32, (8, 128), 0)
    for v in range(4):
        at = slice(128 * v, 128 * v + 128)
        here = pooled[8 * v : 8 * v + 8]
        coarse_ref[:, at] = here
        turned = jnp.where(row < 3, pltpu.roll(here, 5, 0), pltpu.roll(here, 3, 0))
        upper = jnp.where(row < 3, here, turned)
        lower = jnp.where(row < 3, turned, here)
        message = jnp.where(row < 3, e * e * upper + e * lower, e * upper + e * e * lower)
        message = jnp.where(row < 6, message, 0.0)
        for q in range(copies_ref.shape[0] // 8):
            copies_ref[8 * q : 8 * q + 8, at] = message


def edge_kernel(mix_ref, x_ref, low_ref, high_ref, w_ref, main_ref, c_ref, wide, stack):
    cols = x_ref.shape[-1]
    near, far, tile = tile_place()
    top = tile != 0
    bottom = tile != lax.axis_size("near") * lax.axis_size("far") - 1
    stack[144:160, :] = jnp.ones((16, cols), bf16)
    c_ref[:, 14:16, :] = jnp.zeros((3, 2, cols), f32)
    for p in range(3):
        wide[0:5, :] = low_ref[p]
        wide[5:13, :] = x_ref[p]
        wide[13:16, :] = jnp.zeros((3, cols), f32)

        def store_above(at, total):
            c_ref[p, 0:3, at] = jnp.where(top, total[0:3], 0.0)

        paint_window(w_ref, mix_ref, stack, wide[...], store_above)
        wide[0:7, :] = x_ref[p, 1:8, :]
        wide[7:12, :] = high_ref[p]
        wide[12:16, :] = jnp.zeros((4, cols), f32)

        def store_below(at, total):
            c_ref[p, 11:14, at] = jnp.where(bottom, total[5:8], 0.0)

        paint_window(w_ref, mix_ref, stack, wide[...], store_below)
        c_ref[p, 3:11, :] = main_ref[p]


def tile_decay(tiles, used):
    return jnp.where(used, jnp.exp(jnp.maximum(tiles, 0).astype(f32) / -8.0), 0.0)


def runs_kernel(received_ref, total_ref, copies_ref):
    near = lax.axis_index("near")
    count = received_ref.shape[0] // 8
    cols = received_ref.shape[-1]
    forward = lax.broadcasted_iota(jnp.int32, (8, 128), 0) < 3
    totals = [jnp.zeros((8, 128), f32)] * (cols // 128)
    runs = [jnp.zeros((8, 128), f32)] * (cols // 128)
    for q in range(count):
        gap = jnp.where(forward, near - q, q - near) - 1
        weight = tile_decay(gap, gap >= 0)
        to_edge = jnp.where(forward, math.exp(-(count - 1 - q) / 8.0), math.exp(-q / 8.0))
        for v in range(cols // 128):
            value = received_ref[8 * q : 8 * q + 8, 128 * v : 128 * v + 128]
            totals[v] = totals[v] + weight * value
            runs[v] = runs[v] + to_edge * value
    for v in range(cols // 128):
        at = slice(128 * v, 128 * v + 128)
        total_ref[:, at] = totals[v]
        for w in range(copies_ref.shape[0] // 8):
            copies_ref[8 * w : 8 * w + 8, at] = runs[v]


def short_kernel_body(scale, k_ref, c_ref, s_ref, ec_ref, held):
    cols = c_ref.shape[-1]
    for p in range(3):
        held[0:16, :] = c_ref[p]
        held[16:24, :] = jnp.zeros((8, cols), f32)
        for window in range(2):
            total = jnp.zeros((8, cols), f32)
            for b in range(5):
                part = jnp.zeros((8, cols), f32)
                for a in range(5):
                    start = 8 * window + a
                    part = part + k_ref[a, b] * held[start : start + 8, :]
                total = total + (part if b == 2 else shifted(part, b - 2))
            s_ref[p, 8 * window : 8 * window + 8, :] = total
    gap = lax.broadcasted_iota(jnp.int32, ec_ref.shape, 0) - lax.broadcasted_iota(jnp.int32, ec_ref.shape, 1)
    ec_ref[...] = jnp.exp(-jnp.abs(gap.astype(f32)) / scale)


def side_matrix(back):
    shape = (128, 128)
    i = lax.broadcasted_iota(jnp.int32, shape, 1 if back else 0)
    j = lax.broadcasted_iota(jnp.int32, shape, 0 if back else 1)
    return jnp.where(j // 8 == i, jnp.where(i < 8, 1.0, 0.0), 0.0)


def own_lane():
    shape = (8, 128)
    lane = lax.broadcasted_iota(jnp.int32, shape, 1)
    return (lane < 64) & (lane % 8 == lax.broadcasted_iota(jnp.int32, shape, 0))


def bend_kernel(decay, gain, s_ref, coarse_ref, total_ref, run_ref, ec_ref, sent_ref, pot_ref, rows, rim):
    cols = s_ref.shape[-1]
    e = decay
    near, far, tile = tile_place()
    near_count = lax.axis_size("near")
    forward = lax.broadcasted_iota(jnp.int32, (8, rows.shape[-1]), 0) < 3
    acc = total_ref[...]
    inside = jnp.where(forward, near, near_count - 1 - near)
    for w in range(run_ref.shape[0] // 8):
        gap = jnp.where(forward, far - w, w - far) - 1
        acc = acc + tile_decay(gap * near_count + inside, gap >= 0) * run_ref[8 * w : 8 * w + 8, :]
    c0, c1 = coarse_ref[0:3, :], coarse_ref[3:6, :]
    up, down = acc[0:3, :], acc[3:6, :]
    rows[12:16, :] = jnp.zeros((4, rows.shape[-1]), f32)
    rows[0:3, :] = e * c0 + e * e * c1 + e * e * down + up * (1.0 / e)
    rows[3:6, :] = c0 + e * c1 + up + e * down
    rows[6:9, :] = c1 + e * c0 + e * up + down
    rows[9:12, :] = e * e * c0 + e * c1 + e * e * up + down * (1.0 / e)
    smooth = gain * jnp.dot(rows[...], ec_ref[...], precision=highest, preferred_element_type=f32)
    stacked = jnp.concatenate([smooth[:, 128 * v : 128 * v + 128] for v in range(4)], axis=0)
    shape = (128, 512)
    group = lax.broadcasted_iota(jnp.int32, shape, 1) // 4
    grow = jnp.where(group == lax.broadcasted_iota(jnp.int32, shape, 0), 1.0, 0.0)
    grown = jnp.dot(stacked, grow, precision=highest, preferred_element_type=f32)
    long = jnp.concatenate([grown[16 * v : 16 * v + 16] for v in range(4)], axis=1)
    row = lax.broadcasted_iota(jnp.int32, (8, cols), 0)
    lane = lax.broadcasted_iota(jnp.int32, (8, cols), 1) % 128
    top = tile != 0
    bottom = tile != near_count * lax.axis_size("far") - 1
    rim[6:8, :] = jnp.zeros((2, cols), f32)
    side = jnp.zeros((8, cols), f32)
    for p in range(3):
        part = s_ref[p]
        wide = jnp.where(
            row < 4,
            jnp.broadcast_to(long[3 + p : 4 + p], (8, cols)),
            jnp.broadcast_to(long[6 + p : 7 + p], (8, cols)),
        )
        here = part[1:9] + wide
        above_row = jnp.where(top, part[0:1] + long[p : p + 1], 0.0)
        below_row = jnp.where(bottom, part[9:10] + long[9 + p : 10 + p], 0.0)
        pot_ref[p, 7:8, :] = above_row
        pot_ref[p, 8:16, :] = here
        pot_ref[p, 16:17, :] = below_row
        rim[p : p + 1, :] = above_row
        rim[3 + p : 4 + p, :] = below_row
        side = jnp.where(lane == 2 * p, shifted(here, -1 - 2 * p), side)
        side = jnp.where(lane == 2 * p + 1, shifted(here, 127 - 2 * p), side)
        for d in range(cols // 128):
            at = slice(128 * d, 128 * d + 128)
            sent_ref[4 * d + p] = here[:, at]
    rim_rows = rim[...]
    side = jnp.where(lane == 6, shifted(rim_rows, -7), side)
    side = jnp.where(lane == 7, shifted(rim_rows, 121), side)
    blocks = cols // 128
    spread = side_matrix(False)
    lined = jnp.concatenate([side[:, 128 * d : 128 * d + 128] for d in range(blocks)], axis=0)
    lined = jnp.dot(lined, spread, precision=highest, preferred_element_type=f32)
    own = own_lane()
    row = lax.broadcasted_iota(jnp.int32, (8, 128), 0)
    for d in range(blocks):
        line = jnp.sum(jnp.where(own, lined[8 * d : 8 * d + 8], 0.0), axis=0, keepdims=True)
        line = jnp.broadcast_to(line, (8, 128))
        sent_ref[4 * d + 3] = jnp.where(row == 6, line, rim_rows[:, 128 * d : 128 * d + 128])


def own_hessian(pot_ref, u_ref):
    cols = pot_ref.shape[-1]
    for p in range(3):
        here = pot_ref[p, 8:16, :]
        above, below = pot_ref[p, 7:15, :], pot_ref[p, 9:17, :]
        u11 = below - 2.0 * here + above
        u22 = shifted(here, 1) - 2.0 * here + shifted(here, -1)
        step = below - above
        u12 = (shifted(step, 1) - shifted(step, -1)) * 0.25
        for d in range(cols // 128):
            at = slice(128 * d, 128 * d + 128)
            u_ref[9 * d + 3 * p] = u11[:, at]
            u_ref[9 * d + 3 * p + 1] = u12[:, at]
            u_ref[9 * d + 3 * p + 2] = u22[:, at]


def advance(previous, current, u11, u12, u22, mixing, bending):
    kept = 1.0 - mixing
    bent = (
        u11 * current[0] + u12 * current[2],
        u11 * current[1] + u12 * current[3],
        u12 * current[0] + u22 * current[2],
        u12 * current[1] + u22 * current[3],
    )
    return tuple(kept * previous[i] + mixing * current[i] - bending * bent[i] for i in range(4))


def beside(value, left, right):
    lane = lax.broadcasted_iota(jnp.int32, value.shape, 1)
    before = jnp.where(lane == 0, jnp.broadcast_to(left, value.shape), pltpu.roll(value, 1, 1))
    after = jnp.where(lane == 127, jnp.broadcast_to(right, value.shape), pltpu.roll(value, 127, 1))
    return before, after


def over_rows(value, above, below):
    row = lax.broadcasted_iota(jnp.int32, value.shape, 0)
    before = jnp.where(row == 0, jnp.broadcast_to(above, value.shape), pltpu.roll(value, 1, 0))
    after = jnp.where(row == 7, jnp.broadcast_to(below, value.shape), pltpu.roll(value, 7, 0))
    return before, after


def scan_kernel(mixing_ref, bending_ref, sent_ref, pot_ref, state_ref, u_ref):
    own_hessian(pot_ref, u_ref)
    one = jnp.ones((8, 128), f32)
    zero = jnp.zeros((8, 128), f32)
    groups = sent_ref.shape[0] // 4
    own = own_lane()
    at = [(g % 4) * (groups // 4) + g // 4 for g in range(groups)]
    lines = [jnp.broadcast_to(sent_ref[4 * at[g] + 3, 6:7, :], (8, 128)) for g in range(groups)]
    lined = jnp.concatenate([jnp.where(own, line, 0.0) for line in lines], axis=0)
    sides = jnp.dot(lined, side_matrix(True), precision=highest, preferred_element_type=f32)

    previous = current = (one, zero, zero, one)
    for g in range(groups):
        for i in range(4):
            state_ref[8 * at[g] + i] = previous[i]
            state_ref[8 * at[g] + 4 + i] = current[i]
        rim = sent_ref[4 * at[g] + 3]
        side = sides[8 * g : 8 * g + 8]
        rim_left, rim_right = beside(rim, side[:, 6:7], side[:, 7:8])
        rim_step = rim_right - rim_left
        for p in range(3):
            k = 3 * g + p
            here = sent_ref[4 * at[g] + p]
            above, below = over_rows(here, rim[p : p + 1], rim[3 + p : 4 + p])
            left, right = beside(here, side[:, 2 * p : 2 * p + 1], side[:, 2 * p + 1 : 2 * p + 2])
            u11 = below - 2.0 * here + above
            u22 = right - 2.0 * here + left
            step_above, step_below = over_rows(right - left, rim_step[p : p + 1], rim_step[3 + p : 4 + p])
            u12 = (step_below - step_above) * 0.25
            later = advance(previous, current, u11, u12, u22, mixing_ref[k], bending_ref[k])
            previous, current = current, later


def final_kernel(mixing_ref, bending_ref, u_ref, state_ref, out_ref):
    blocks = u_ref.shape[0] // 9
    first = 3 * (lax.axis_size("z") * lax.axis_index("x") + lax.axis_index("z"))

    def one_block(d, carry):
        at = pl.ds(pl.multiple_of(d * 128, 128), 128)
        previous = tuple(state_ref[8 * d + i] for i in range(4))
        current = tuple(state_ref[8 * d + 4 + i] for i in range(4))
        for p in range(3):
            k = 9 * d + 3 * p
            later = advance(
                previous,
                current,
                u_ref[k],
                u_ref[k + 1],
                u_ref[k + 2],
                mixing_ref[first + p],
                bending_ref[first + p],
            )
            for i in range(4):
                out_ref[i, p, :, at] = later[i]
            previous, current = current, later
        return carry

    lax.fori_loop(0, blocks, one_block, 0, unroll=True)


vmem = pl.BlockSpec(memory_space=pltpu.VMEM)
smem = pl.BlockSpec(memory_space=pltpu.SMEM)


def sds(*shape):
    return jax.ShapeDtypeStruct(shape, f32)


def call(kernel, name, n_smem, n_vmem, out_shape, scratch=(), cost=(0, 0, 0)):
    outs = jax.tree.map(lambda _: vmem, out_shape)
    return pl.pallas_call(
        kernel,
        name=name,
        out_shape=out_shape,
        in_specs=[smem] * n_smem + [vmem] * n_vmem,
        out_specs=outs,
        scratch_shapes=list(scratch),
        cost_estimate=pl.CostEstimate(flops=cost[0], bytes_accessed=cost[1], transcendentals=cost[2]),
        compiler_params=pltpu.CompilerParams(vmem_limit_bytes=24 << 20),
    )


def body(density, plane_slot, paint_weight, paint_bias, mix_weight, short_kernel):
    plane_count, row_count, col_count = density.shape
    tile = ("far", "near")
    near_count, far_count = lax.axis_size("near"), lax.axis_size("far")
    tile_count = far_count * near_count
    group_count = lax.axis_size("x") * lax.axis_size("z")
    coarse_cols = col_count // 4
    row_scale = row_count * tile_count / 16.0
    col_scale = col_count / 16.0
    long_gain = 1.0 / math.sqrt(row_scale * col_scale)
    decay = math.exp(-1.0 / row_scale)

    up = [(i, i + 1) for i in range(tile_count - 1)]
    low = lax.ppermute(density[:, 3:8, :], tile, up)
    high = lax.ppermute(density[:, 0:5, :], tile, [(b, a) for a, b in up])

    scalars = jnp.concatenate([paint_bias, mix_weight])
    weights, pool = call(
        weights_kernel,
        "weights",
        2,
        0,
        (jax.ShapeDtypeStruct((channels * 8, 160), bf16), sds(col_count // 4, col_count // 16)),
        (),
        (10**6, 10**5, 0),
    )(paint_weight, scalars)
    mixing, bending = distances(plane_slot, 2 * plane_slot.shape[0])
    main, coarse, copies = call(
        functools.partial(paint_kernel, decay),
        "paint",
        1,
        5,
        (
            sds(plane_count, row_count, col_count),
            sds(8, coarse_cols),
            sds(8 * near_count, coarse_cols),
        ),
        [pltpu.VMEM((16, col_count), f32), pltpu.VMEM((160, col_count), bf16), pltpu.VMEM((8, col_count), f32)],
        (4 * 10**9, 2 * 10**6, 10**6),
    )(scalars, density, low, high, weights, pool)
    copies, mixing, bending = lax.optimization_barrier((copies, mixing, bending))

    received = lax.all_to_all(copies, "near", 0, 0, tiled=True)
    convergence = call(
        edge_kernel,
        "edges",
        1,
        5,
        sds(plane_count, 16, col_count),
        [pltpu.VMEM((16, col_count), f32), pltpu.VMEM((160, col_count), bf16)],
        (8 * 10**9, 2 * 10**6, 10**6),
    )(scalars, density, low, high, weights, main)
    total, run_copies = call(
        runs_kernel, "runs", 0, 1, (sds(8, coarse_cols), sds(8 * far_count, coarse_cols)), (), (10**6, 10**5, 0)
    )(received)
    convergence, run_copies = lax.optimization_barrier((convergence, run_copies))
    runs = lax.all_to_all(run_copies, "far", 0, 0, tiled=True)
    short_part, col_kernel = call(
        functools.partial(short_kernel_body, col_scale),
        "short",
        1,
        1,
        (sds(plane_count, 16, col_count), sds(coarse_cols, coarse_cols)),
        [pltpu.VMEM((24, col_count), f32)],
        (10**7, 10**6, 0),
    )(short_kernel, convergence)

    sent, potential = call(
        functools.partial(bend_kernel, decay, long_gain),
        "bend",
        0,
        5,
        (sds(group_count * 4, 8, 128), sds(plane_count, 24, col_count)),
        [pltpu.VMEM((16, coarse_cols), f32), pltpu.VMEM((8, col_count), f32)],
        (10**8, 2 * 10**6, 0),
    )(short_part, coarse, total, runs, col_kernel)

    gathered = lax.all_to_all(sent, ("z", "x"), 0, 0, tiled=True)
    states, shear = call(
        scan_kernel,
        "scan",
        2,
        2,
        (sds(group_count * 8, 8, 128), sds(group_count * 9, 8, 128)),
        (),
        (10**7, 10**6, 0),
    )(mixing, bending, gathered, potential)
    mine = lax.all_to_all(states, ("z", "x"), 0, 0, tiled=True)
    return call(final_kernel, "final", 2, 2, sds(4, plane_count, row_count, col_count), (), (10**7, 10**6, 0))(
        mixing, bending, shear, mine
    )


def solution(mesh):
    planes, tiles = mesh.devices.shape
    split = Mesh(mesh.devices.reshape(planes // 4, 4, 4, tiles // 4), ("x", "z", "far", "near"))
    tile = ("far", "near")
    plane = ("x", "z")
    placed = (P(plane, tile, None), P(), P(), P(), P(), P())
    return jax.shard_map(
        body, mesh=split, in_specs=placed, out_specs=P(None, plane, tile, None), check_vma=False
    )
```

```python
import functools
import math

import jax
import jax.numpy as jnp
from jax import lax
from jax.experimental import pallas as pl
from jax.experimental.pallas import tpu as pltpu
from jax.sharding import Mesh
from jax.sharding import PartitionSpec as P

f32 = jnp.float32
bf16 = jnp.bfloat16
lens_gain = 0.25
channels = 32
highest = lax.Precision.HIGHEST


def distances(plane_slot, slot_total):
    distance = (plane_slot.astype(f32) + 1.0) / slot_total
    before = jnp.concatenate([jnp.zeros((1,), f32), distance[:-1]])
    after = jnp.concatenate([distance[1:], jnp.full((1,), (slot_total + 1.0) / slot_total, f32)])
    mixing = before * (after - distance) / (distance * (after - before))
    bending = lens_gain * (after - distance) / after
    return (mixing, bending)


def shifted(value, by):
    width = value.shape[-1]
    rolled = pltpu.roll(value, (-by) % width, value.ndim - 1)
    lane = lax.broadcasted_iota(jnp.int32, value.shape, value.ndim - 1)
    keep = lane < width - by if by > 0 else lane >= -by
    return jnp.where(keep, rolled, 0.0)


def tile_place():
    near, far = lax.axis_index("near"), lax.axis_index("far")
    return near, far, far * lax.axis_size("near") + near


def weights_kernel(w_ref, b_ref, out_ref, pool_ref):
    group = lax.broadcasted_iota(jnp.int32, pool_ref.shape, 0) // 4
    pool_ref[...] = jnp.where(group == lax.broadcasted_iota(jnp.int32, pool_ref.shape, 1), 1.0 / 16.0, 0.0)
    shape = (8, 160)
    row = lax.broadcasted_iota(jnp.int32, shape, 0)
    col = lax.broadcasted_iota(jnp.int32, shape, 1)
    part, in_row = col // 16, col % 16
    taps = []
    for i in range(3):
        for j in range(3):
            here = (in_row == row + 2 * i) & (part % 3 == j) & (part < 9)
            taps.append(jnp.where(here, 1.0, 0.0))
    bias_here = jnp.where((col >= 144) & (col < 147), 1.0, 0.0)
    for c in range(channels):
        exact = b_ref[c] * bias_here
        for t in range(9):
            exact = exact + w_ref[c, t] * taps[t]
        first = exact.astype(bf16).astype(f32)
        second = (exact - first).astype(bf16).astype(f32)
        third = exact - first - second
        value = jnp.where((col < 96) | (col == 144), first, jnp.where(col < 146, second, third))
        out_ref[8 * c : 8 * c + 8, :] = value.astype(bf16)


def paint_window(w_ref, mix_ref, stack, value, store):
    cols = value.shape[-1]
    for j in range(3):
        moved = value if j == 1 else shifted(value, 2 * (j - 1))
        upper = moved.astype(bf16)
        lower = (moved - upper.astype(f32)).astype(bf16)
        stack[16 * j : 16 * j + 16, :] = upper
        stack[48 + 16 * j : 64 + 16 * j, :] = lower
        stack[96 + 16 * j : 112 + 16 * j, :] = upper

    def one_chunk(chunk, carry):
        at = pl.ds(pl.multiple_of(chunk * 256, 256), 256)
        before = jnp.dot(w_ref[...], stack[:, at], preferred_element_type=f32)
        total = jnp.zeros((8, 256), f32)
        for c in range(channels):
            total = total + mix_ref[channels + c] * jnp.tanh(before[8 * c : 8 * c + 8, :])
        store(at, total)
        return carry

    lax.fori_loop(0, cols // 256, one_chunk, 0, unroll=True)


def paint_kernel(decay, mix_ref, x_ref, mate_ref, other_ref, w_ref, pool_ref, c_ref, coarse_ref, copies_ref, wide, stack, sums):
    cols = x_ref.shape[-1]
    wide[12:16, :] = jnp.zeros((4, cols), f32)
    sums[6:8, :] = jnp.zeros((2, cols), f32)
    stack[144:160, :] = jnp.ones((16, cols), bf16)
    for p in range(3):
        low, high = beside_rows(mate_ref, other_ref, p)
        wide[0:2, :] = low[3:5]
        wide[2:10, :] = x_ref[p]
        wide[10:12, :] = high[0:2]

        def store(at, total):
            c_ref[p, :, at] = total
            sums[p : p + 1, at] = jnp.sum(total[0:4], axis=0, keepdims=True)
            sums[3 + p : 4 + p, at] = jnp.sum(total[4:8], axis=0, keepdims=True)

        paint_window(w_ref, mix_ref, stack, wide[...], store)
    quarter = cols // 4
    stacked = jnp.concatenate([sums[:, quarter * v : quarter * (v + 1)] for v in range(4)], axis=0)
    pooled = jnp.dot(stacked, pool_ref[...], precision=highest, preferred_element_type=f32)
    e = decay
    row = lax.broadcasted_iota(jnp.int32, (8, 128), 0)
    for v in range(4):
        at = slice(128 * v, 128 * v + 128)
        here = pooled[8 * v : 8 * v + 8]
        coarse_ref[:, at] = here
        turned = jnp.where(row < 3, pltpu.roll(here, 5, 0), pltpu.roll(here, 3, 0))
        upper = jnp.where(row < 3, here, turned)
        lower = jnp.where(row < 3, turned, here)
        message = jnp.where(row < 3, e * e * upper + e * lower, e * upper + e * e * lower)
        message = jnp.where(row < 6, message, 0.0)
        for q in range(copies_ref.shape[0] // 8):
            copies_ref[8 * q : 8 * q + 8, at] = message


def edge_kernel(mix_ref, x_ref, mate_ref, other_ref, w_ref, main_ref, c_ref, wide, stack):
    cols = x_ref.shape[-1]
    near, far, tile = tile_place()
    top = tile != 0
    bottom = tile != lax.axis_size("near") * lax.axis_size("far") - 1
    stack[144:160, :] = jnp.ones((16, cols), bf16)
    c_ref[:, 14:16, :] = jnp.zeros((3, 2, cols), f32)
    for p in range(3):
        low, high = beside_rows(mate_ref, other_ref, p)
        wide[0:5, :] = low
        wide[5:13, :] = x_ref[p]
        wide[13:16, :] = jnp.zeros((3, cols), f32)

        def store_above(at, total):
            c_ref[p, 0:3, at] = jnp.where(top, total[0:3], 0.0)

        paint_window(w_ref, mix_ref, stack, wide[...], store_above)
        wide[0:7, :] = x_ref[p, 1:8, :]
        wide[7:12, :] = high
        wide[12:16, :] = jnp.zeros((4, cols), f32)

        def store_below(at, total):
            c_ref[p, 11:14, at] = jnp.where(bottom, total[5:8], 0.0)

        paint_window(w_ref, mix_ref, stack, wide[...], store_below)
        c_ref[p, 3:11, :] = main_ref[p]


def beside_rows(mate_ref, other_ref, p):
    even = lax.axis_index("near") % 2 == 0
    mate, other = mate_ref[p], other_ref[p]
    return jnp.where(even, other, mate), jnp.where(even, mate, other)


def tile_decay(tiles, used):
    return jnp.where(used, jnp.exp(jnp.maximum(tiles, 0).astype(f32) / -8.0), 0.0)


def runs_kernel(received_ref, total_ref, copies_ref):
    near = lax.axis_index("near")
    count = received_ref.shape[0] // 8
    cols = received_ref.shape[-1]
    forward = lax.broadcasted_iota(jnp.int32, (8, 128), 0) < 3
    totals = [jnp.zeros((8, 128), f32)] * (cols // 128)
    runs = [jnp.zeros((8, 128), f32)] * (cols // 128)
    for q in range(count):
        gap = jnp.where(forward, near - q, q - near) - 1
        weight = tile_decay(gap, gap >= 0)
        to_edge = jnp.where(forward, math.exp(-(count - 1 - q) / 8.0), math.exp(-q / 8.0))
        for v in range(cols // 128):
            value = received_ref[8 * q : 8 * q + 8, 128 * v : 128 * v + 128]
            totals[v] = totals[v] + weight * value
            runs[v] = runs[v] + to_edge * value
    for v in range(cols // 128):
        at = slice(128 * v, 128 * v + 128)
        total_ref[:, at] = totals[v]
        for w in range(copies_ref.shape[0] // 8):
            copies_ref[8 * w : 8 * w + 8, at] = runs[v]


def short_kernel_body(scale, k_ref, c_ref, s_ref, ec_ref, held):
    cols = c_ref.shape[-1]
    for p in range(3):
        held[0:16, :] = c_ref[p]
        held[16:24, :] = jnp.zeros((8, cols), f32)
        for window in range(2):
            total = jnp.zeros((8, cols), f32)
            for b in range(5):
                part = jnp.zeros((8, cols), f32)
                for a in range(5):
                    start = 8 * window + a
                    part = part + k_ref[a, b] * held[start : start + 8, :]
                total = total + (part if b == 2 else shifted(part, b - 2))
            s_ref[p, 8 * window : 8 * window + 8, :] = total
    gap = lax.broadcasted_iota(jnp.int32, ec_ref.shape, 0) - lax.broadcasted_iota(jnp.int32, ec_ref.shape, 1)
    ec_ref[...] = jnp.exp(-jnp.abs(gap.astype(f32)) / scale)


def side_matrix(back):
    shape = (128, 128)
    i = lax.broadcasted_iota(jnp.int32, shape, 1 if back else 0)
    j = lax.broadcasted_iota(jnp.int32, shape, 0 if back else 1)
    return jnp.where(j // 8 == i, jnp.where(i < 8, 1.0, 0.0), 0.0)


def own_lane():
    shape = (8, 128)
    lane = lax.broadcasted_iota(jnp.int32, shape, 1)
    return (lane < 64) & (lane % 8 == lax.broadcasted_iota(jnp.int32, shape, 0))


def bend_kernel(decay, gain, s_ref, coarse_ref, total_ref, run_ref, ec_ref, sent_ref, pot_ref, rows, rim):
    cols = s_ref.shape[-1]
    e = decay
    near, far, tile = tile_place()
    near_count = lax.axis_size("near")
    forward = lax.broadcasted_iota(jnp.int32, (8, rows.shape[-1]), 0) < 3
    acc = total_ref[...]
    inside = jnp.where(forward, near, near_count - 1 - near)
    for w in range(run_ref.shape[0] // 8):
        gap = jnp.where(forward, far - w, w - far) - 1
        acc = acc + tile_decay(gap * near_count + inside, gap >= 0) * run_ref[8 * w : 8 * w + 8, :]
    c0, c1 = coarse_ref[0:3, :], coarse_ref[3:6, :]
    up, down = acc[0:3, :], acc[3:6, :]
    rows[12:16, :] = jnp.zeros((4, rows.shape[-1]), f32)
    rows[0:3, :] = e * c0 + e * e * c1 + e * e * down + up * (1.0 / e)
    rows[3:6, :] = c0 + e * c1 + up + e * down
    rows[6:9, :] = c1 + e * c0 + e * up + down
    rows[9:12, :] = e * e * c0 + e * c1 + e * e * up + down * (1.0 / e)
    smooth = gain * jnp.dot(rows[...], ec_ref[...], precision=highest, preferred_element_type=f32)
    stacked = jnp.concatenate([smooth[:, 128 * v : 128 * v + 128] for v in range(4)], axis=0)
    shape = (128, 512)
    group = lax.broadcasted_iota(jnp.int32, shape, 1) // 4
    grow = jnp.where(group == lax.broadcasted_iota(jnp.int32, shape, 0), 1.0, 0.0)
    grown = jnp.dot(stacked, grow, precision=highest, preferred_element_type=f32)
    long = jnp.concatenate([grown[16 * v : 16 * v + 16] for v in range(4)], axis=1)
    row = lax.broadcasted_iota(jnp.int32, (8, cols), 0)
    lane = lax.broadcasted_iota(jnp.int32, (8, cols), 1) % 128
    top = tile != 0
    bottom = tile != near_count * lax.axis_size("far") - 1
    rim[6:8, :] = jnp.zeros((2, cols), f32)
    side = jnp.zeros((8, cols), f32)
    for p in range(3):
        part = s_ref[p]
        wide = jnp.where(
            row < 4,
            jnp.broadcast_to(long[3 + p : 4 + p], (8, cols)),
            jnp.broadcast_to(long[6 + p : 7 + p], (8, cols)),
        )
        here = part[1:9] + wide
        above_row = jnp.where(top, part[0:1] + long[p : p + 1], 0.0)
        below_row = jnp.where(bottom, part[9:10] + long[9 + p : 10 + p], 0.0)
        pot_ref[p, 7:8, :] = above_row
        pot_ref[p, 8:16, :] = here
        pot_ref[p, 16:17, :] = below_row
        rim[p : p + 1, :] = above_row
        rim[3 + p : 4 + p, :] = below_row
        side = jnp.where(lane == 2 * p, shifted(here, -1 - 2 * p), side)
        side = jnp.where(lane == 2 * p + 1, shifted(here, 127 - 2 * p), side)
        for d in range(cols // 128):
            at = slice(128 * d, 128 * d + 128)
            sent_ref[4 * d + p] = here[:, at]
    rim_rows = rim[...]
    side = jnp.where(lane == 6, shifted(rim_rows, -7), side)
    side = jnp.where(lane == 7, shifted(rim_rows, 121), side)
    blocks = cols // 128
    spread = side_matrix(False)
    lined = jnp.concatenate([side[:, 128 * d : 128 * d + 128] for d in range(blocks)], axis=0)
    lined = jnp.dot(lined, spread, precision=highest, preferred_element_type=f32)
    own = own_lane()
    row = lax.broadcasted_iota(jnp.int32, (8, 128), 0)
    for d in range(blocks):
        line = jnp.sum(jnp.where(own, lined[8 * d : 8 * d + 8], 0.0), axis=0, keepdims=True)
        line = jnp.broadcast_to(line, (8, 128))
        sent_ref[4 * d + 3] = jnp.where(row == 6, line, rim_rows[:, 128 * d : 128 * d + 128])


def own_hessian(pot_ref, u_ref):
    cols = pot_ref.shape[-1]
    for p in range(3):
        here = pot_ref[p, 8:16, :]
        above, below = pot_ref[p, 7:15, :], pot_ref[p, 9:17, :]
        u11 = below - 2.0 * here + above
        u22 = shifted(here, 1) - 2.0 * here + shifted(here, -1)
        step = below - above
        u12 = (shifted(step, 1) - shifted(step, -1)) * 0.25
        for d in range(cols // 128):
            at = slice(128 * d, 128 * d + 128)
            u_ref[9 * d + 3 * p] = u11[:, at]
            u_ref[9 * d + 3 * p + 1] = u12[:, at]
            u_ref[9 * d + 3 * p + 2] = u22[:, at]


def advance(previous, current, u11, u12, u22, mixing, bending):
    kept = 1.0 - mixing
    bent = (
        u11 * current[0] + u12 * current[2],
        u11 * current[1] + u12 * current[3],
        u12 * current[0] + u22 * current[2],
        u12 * current[1] + u22 * current[3],
    )
    return tuple(kept * previous[i] + mixing * current[i] - bending * bent[i] for i in range(4))


def beside(value, left, right):
    lane = lax.broadcasted_iota(jnp.int32, value.shape, 1)
    before = jnp.where(lane == 0, jnp.broadcast_to(left, value.shape), pltpu.roll(value, 1, 1))
    after = jnp.where(lane == 127, jnp.broadcast_to(right, value.shape), pltpu.roll(value, 127, 1))
    return before, after


def over_rows(value, above, below):
    row = lax.broadcasted_iota(jnp.int32, value.shape, 0)
    before = jnp.where(row == 0, jnp.broadcast_to(above, value.shape), pltpu.roll(value, 1, 0))
    after = jnp.where(row == 7, jnp.broadcast_to(below, value.shape), pltpu.roll(value, 7, 0))
    return before, after


def scan_kernel(mixing_ref, bending_ref, sent_ref, pot_ref, state_ref, u_ref):
    own_hessian(pot_ref, u_ref)
    one = jnp.ones((8, 128), f32)
    zero = jnp.zeros((8, 128), f32)
    groups = sent_ref.shape[0] // 4
    own = own_lane()
    at = [(g % 4) * (groups // 4) + g // 4 for g in range(groups)]
    lines = [jnp.broadcast_to(sent_ref[4 * at[g] + 3, 6:7, :], (8, 128)) for g in range(groups)]
    lined = jnp.concatenate([jnp.where(own, line, 0.0) for line in lines], axis=0)
    sides = jnp.dot(lined, side_matrix(True), precision=highest, preferred_element_type=f32)

    previous = current = (one, zero, zero, one)
    for g in range(groups):
        for i in range(4):
            state_ref[8 * at[g] + i] = previous[i]
            state_ref[8 * at[g] + 4 + i] = current[i]
        rim = sent_ref[4 * at[g] + 3]
        side = sides[8 * g : 8 * g + 8]
        rim_left, rim_right = beside(rim, side[:, 6:7], side[:, 7:8])
        rim_step = rim_right - rim_left
        for p in range(3):
            k = 3 * g + p
            here = sent_ref[4 * at[g] + p]
            above, below = over_rows(here, rim[p : p + 1], rim[3 + p : 4 + p])
            left, right = beside(here, side[:, 2 * p : 2 * p + 1], side[:, 2 * p + 1 : 2 * p + 2])
            u11 = below - 2.0 * here + above
            u22 = right - 2.0 * here + left
            step_above, step_below = over_rows(right - left, rim_step[p : p + 1], rim_step[3 + p : 4 + p])
            u12 = (step_below - step_above) * 0.25
            later = advance(previous, current, u11, u12, u22, mixing_ref[k], bending_ref[k])
            previous, current = current, later


def final_kernel(mixing_ref, bending_ref, u_ref, state_ref, out_ref):
    blocks = u_ref.shape[0] // 9
    first = 3 * (lax.axis_size("z") * lax.axis_index("x") + lax.axis_index("z"))

    def one_block(d, carry):
        at = pl.ds(pl.multiple_of(d * 128, 128), 128)
        previous = tuple(state_ref[8 * d + i] for i in range(4))
        current = tuple(state_ref[8 * d + 4 + i] for i in range(4))
        for p in range(3):
            k = 9 * d + 3 * p
            later = advance(
                previous,
                current,
                u_ref[k],
                u_ref[k + 1],
                u_ref[k + 2],
                mixing_ref[first + p],
                bending_ref[first + p],
            )
            for i in range(4):
                out_ref[i, p, :, at] = later[i]
            previous, current = current, later
        return carry

    lax.fori_loop(0, blocks, one_block, 0, unroll=True)


vmem = pl.BlockSpec(memory_space=pltpu.VMEM)
smem = pl.BlockSpec(memory_space=pltpu.SMEM)


def sds(*shape):
    return jax.ShapeDtypeStruct(shape, f32)


def call(kernel, name, n_smem, n_vmem, out_shape, scratch=(), cost=(0, 0, 0)):
    outs = jax.tree.map(lambda _: vmem, out_shape)
    return pl.pallas_call(
        kernel,
        name=name,
        out_shape=out_shape,
        in_specs=[smem] * n_smem + [vmem] * n_vmem,
        out_specs=outs,
        scratch_shapes=list(scratch),
        cost_estimate=pl.CostEstimate(flops=cost[0], bytes_accessed=cost[1], transcendentals=cost[2]),
        compiler_params=pltpu.CompilerParams(vmem_limit_bytes=24 << 20),
    )


def body(density, plane_slot, paint_weight, paint_bias, mix_weight, short_kernel):
    plane_count, row_count, col_count = density.shape
    tile = ("far", "near")
    near_index = lax.axis_index("near")
    near_count, far_count = lax.axis_size("near"), lax.axis_size("far")
    tile_count = far_count * near_count
    group_count = lax.axis_size("x") * lax.axis_size("z")
    coarse_cols = col_count // 4
    row_scale = row_count * tile_count / 16.0
    col_scale = col_count / 16.0
    long_gain = 1.0 / math.sqrt(row_scale * col_scale)
    decay = math.exp(-1.0 / row_scale)

    even = near_index % 2 == 0
    last_rows, first_rows = density[:, 3:8, :], density[:, 0:5, :]
    pairs = [(i, i ^ 1) for i in range(tile_count)]
    mate = lax.ppermute(jnp.where(even, last_rows, first_rows), tile, pairs)
    pairs = [(i, ((i + 1) ^ 1) - 1) for i in range(1, tile_count - 1)]
    other = lax.ppermute(jnp.where(even, first_rows, last_rows), tile, pairs)

    scalars = jnp.concatenate([paint_bias, mix_weight])
    weights, pool = call(
        weights_kernel,
        "weights",
        2,
        0,
        (jax.ShapeDtypeStruct((channels * 8, 160), bf16), sds(col_count // 4, col_count // 16)),
        (),
        (10**6, 10**5, 0),
    )(paint_weight, scalars)
    mixing, bending = distances(plane_slot, 2 * plane_slot.shape[0])
    main, coarse, copies = call(
        functools.partial(paint_kernel, decay),
        "paint",
        1,
        5,
        (
            sds(plane_count, row_count, col_count),
            sds(8, coarse_cols),
            sds(8 * near_count, coarse_cols),
        ),
        [pltpu.VMEM((16, col_count), f32), pltpu.VMEM((160, col_count), bf16), pltpu.VMEM((8, col_count), f32)],
        (4 * 10**9, 2 * 10**6, 10**6),
    )(scalars, density, mate, other, weights, pool)
    copies, mixing, bending = lax.optimization_barrier((copies, mixing, bending))

    received = lax.all_to_all(copies, "near", 0, 0, tiled=True)
    convergence = call(
        edge_kernel,
        "edges",
        1,
        5,
        sds(plane_count, 16, col_count),
        [pltpu.VMEM((16, col_count), f32), pltpu.VMEM((160, col_count), bf16)],
        (8 * 10**9, 2 * 10**6, 10**6),
    )(scalars, density, mate, other, weights, main)
    total, run_copies = call(
        runs_kernel, "runs", 0, 1, (sds(8, coarse_cols), sds(8 * far_count, coarse_cols)), (), (10**6, 10**5, 0)
    )(received)
    convergence, run_copies = lax.optimization_barrier((convergence, run_copies))
    runs = lax.all_to_all(run_copies, "far", 0, 0, tiled=True)
    short_part, col_kernel = call(
        functools.partial(short_kernel_body, col_scale),
        "short",
        1,
        1,
        (sds(plane_count, 16, col_count), sds(coarse_cols, coarse_cols)),
        [pltpu.VMEM((24, col_count), f32)],
        (10**7, 10**6, 0),
    )(short_kernel, convergence)

    sent, potential = call(
        functools.partial(bend_kernel, decay, long_gain),
        "bend",
        0,
        5,
        (sds(group_count * 4, 8, 128), sds(plane_count, 24, col_count)),
        [pltpu.VMEM((16, coarse_cols), f32), pltpu.VMEM((8, col_count), f32)],
        (10**8, 2 * 10**6, 0),
    )(short_part, coarse, total, runs, col_kernel)

    gathered = lax.all_to_all(sent, ("z", "x"), 0, 0, tiled=True)
    states, shear = call(
        scan_kernel,
        "scan",
        2,
        2,
        (sds(group_count * 8, 8, 128), sds(group_count * 9, 8, 128)),
        (),
        (10**7, 10**6, 0),
    )(mixing, bending, gathered, potential)
    mine = lax.all_to_all(states, ("z", "x"), 0, 0, tiled=True)
    return call(final_kernel, "final", 2, 2, sds(4, plane_count, row_count, col_count), (), (10**7, 10**6, 0))(
        mixing, bending, shear, mine
    )


def solution(mesh):
    planes, tiles = mesh.devices.shape
    split = Mesh(mesh.devices.reshape(planes // 4, 4, 4, tiles // 4), ("x", "z", "far", "near"))
    tile = ("far", "near")
    plane = ("x", "z")
    placed = (P(plane, tile, None), P(), P(), P(), P(), P())
    return jax.shard_map(
        body, mesh=split, in_specs=placed, out_specs=P(None, plane, tile, None), check_vma=False
    )
```

```python
import functools
import math

import jax
import jax.numpy as jnp
from jax import lax
from jax.experimental import pallas as pl
from jax.experimental.pallas import tpu as pltpu
from jax.sharding import Mesh
from jax.sharding import PartitionSpec as P

f32 = jnp.float32
bf16 = jnp.bfloat16
lens_gain = 0.25
channels = 32
highest = lax.Precision.HIGHEST


def distances(plane_slot, slot_total):
    distance = (plane_slot.astype(f32) + 1.0) / slot_total
    before = jnp.concatenate([jnp.zeros((1,), f32), distance[:-1]])
    after = jnp.concatenate([distance[1:], jnp.full((1,), (slot_total + 1.0) / slot_total, f32)])
    mixing = before * (after - distance) / (distance * (after - before))
    bending = lens_gain * (after - distance) / after
    return (mixing, bending)


def shifted(value, by):
    width = value.shape[-1]
    rolled = pltpu.roll(value, (-by) % width, value.ndim - 1)
    lane = lax.broadcasted_iota(jnp.int32, value.shape, value.ndim - 1)
    keep = lane < width - by if by > 0 else lane >= -by
    return jnp.where(keep, rolled, 0.0)


def tile_place():
    near, far = (2 * lax.axis_index("y") + lax.axis_index("core")), lax.axis_index("far")
    return near, far, far * 8 + near


def weights_kernel(w_ref, b_ref, out_ref, pool_ref):
    group = lax.broadcasted_iota(jnp.int32, pool_ref.shape, 0) // 4
    pool_ref[...] = jnp.where(group == lax.broadcasted_iota(jnp.int32, pool_ref.shape, 1), 1.0 / 16.0, 0.0)
    shape = (8, 160)
    row = lax.broadcasted_iota(jnp.int32, shape, 0)
    col = lax.broadcasted_iota(jnp.int32, shape, 1)
    part, in_row = col // 16, col % 16
    taps = []
    for i in range(3):
        for j in range(3):
            here = (in_row == row + 2 * i) & (part % 3 == j) & (part < 9)
            taps.append(jnp.where(here, 1.0, 0.0))
    bias_here = jnp.where((col >= 144) & (col < 147), 1.0, 0.0)
    for c in range(channels):
        exact = b_ref[c] * bias_here
        for t in range(9):
            exact = exact + w_ref[c, t] * taps[t]
        first = exact.astype(bf16).astype(f32)
        second = (exact - first).astype(bf16).astype(f32)
        third = exact - first - second
        value = jnp.where((col < 96) | (col == 144), first, jnp.where(col < 146, second, third))
        out_ref[8 * c : 8 * c + 8, :] = value.astype(bf16)


def paint_window(w_ref, mix_ref, stack, value, store):
    cols = value.shape[-1]
    for j in range(3):
        moved = value if j == 1 else shifted(value, 2 * (j - 1))
        upper = moved.astype(bf16)
        lower = (moved - upper.astype(f32)).astype(bf16)
        stack[16 * j : 16 * j + 16, :] = upper
        stack[48 + 16 * j : 64 + 16 * j, :] = lower
        stack[96 + 16 * j : 112 + 16 * j, :] = upper

    def one_chunk(chunk, carry):
        at = pl.ds(pl.multiple_of(chunk * 256, 256), 256)
        before = jnp.dot(w_ref[...], stack[:, at], preferred_element_type=f32)
        total = jnp.zeros((8, 256), f32)
        for c in range(channels):
            total = total + mix_ref[channels + c] * jnp.tanh(before[8 * c : 8 * c + 8, :])
        store(at, total)
        return carry

    lax.fori_loop(0, cols // 256, one_chunk, 0, unroll=True)


def paint_kernel(decay, mix_ref, x_ref, mate_ref, other_ref, w_ref, pool_ref, c_ref, coarse_ref, copies_ref, wide, stack, sums):
    cols = x_ref.shape[-1]
    wide[12:16, :] = jnp.zeros((4, cols), f32)
    sums[6:8, :] = jnp.zeros((2, cols), f32)
    stack[144:160, :] = jnp.ones((16, cols), bf16)
    for p in range(3):
        low, high = beside_rows(mate_ref, other_ref, p)
        wide[0:2, :] = low[3:5]
        wide[2:10, :] = x_ref[p]
        wide[10:12, :] = high[0:2]

        def store(at, total):
            c_ref[p, :, at] = total
            sums[p : p + 1, at] = jnp.sum(total[0:4], axis=0, keepdims=True)
            sums[3 + p : 4 + p, at] = jnp.sum(total[4:8], axis=0, keepdims=True)

        paint_window(w_ref, mix_ref, stack, wide[...], store)
    quarter = cols // 4
    stacked = jnp.concatenate([sums[:, quarter * v : quarter * (v + 1)] for v in range(4)], axis=0)
    pooled = jnp.dot(stacked, pool_ref[...], precision=highest, preferred_element_type=f32)
    e = decay
    row = lax.broadcasted_iota(jnp.int32, (8, 128), 0)
    for v in range(4):
        at = slice(128 * v, 128 * v + 128)
        here = pooled[8 * v : 8 * v + 8]
        coarse_ref[:, at] = here
        turned = jnp.where(row < 3, pltpu.roll(here, 5, 0), pltpu.roll(here, 3, 0))
        upper = jnp.where(row < 3, here, turned)
        lower = jnp.where(row < 3, turned, here)
        message = jnp.where(row < 3, e * e * upper + e * lower, e * upper + e * e * lower)
        message = jnp.where(row < 6, message, 0.0)
        for q in range(copies_ref.shape[0] // 8):
            copies_ref[8 * q : 8 * q + 8, at] = message


def edge_kernel(mix_ref, x_ref, mate_ref, other_ref, w_ref, main_ref, c_ref, wide, stack):
    cols = x_ref.shape[-1]
    near, far, tile = tile_place()
    top = tile != 0
    bottom = tile != 8 * lax.axis_size("far") - 1
    stack[144:160, :] = jnp.ones((16, cols), bf16)
    c_ref[:, 14:16, :] = jnp.zeros((3, 2, cols), f32)
    for p in range(3):
        low, high = beside_rows(mate_ref, other_ref, p)
        wide[0:5, :] = low
        wide[5:13, :] = x_ref[p]
        wide[13:16, :] = jnp.zeros((3, cols), f32)

        def store_above(at, total):
            c_ref[p, 0:3, at] = jnp.where(top, total[0:3], 0.0)

        paint_window(w_ref, mix_ref, stack, wide[...], store_above)
        wide[0:7, :] = x_ref[p, 1:8, :]
        wide[7:12, :] = high
        wide[12:16, :] = jnp.zeros((4, cols), f32)

        def store_below(at, total):
            c_ref[p, 11:14, at] = jnp.where(bottom, total[5:8], 0.0)

        paint_window(w_ref, mix_ref, stack, wide[...], store_below)
        c_ref[p, 3:11, :] = main_ref[p]


def beside_rows(mate_ref, other_ref, p):
    even = (2 * lax.axis_index("y") + lax.axis_index("core")) % 2 == 0
    mate, other = mate_ref[p], other_ref[p]
    return jnp.where(even, other, mate), jnp.where(even, mate, other)


def tile_decay(tiles, used):
    return jnp.where(used, jnp.exp(jnp.maximum(tiles, 0).astype(f32) / -8.0), 0.0)


def runs_kernel(received_ref, total_ref, copies_ref):
    near = (2 * lax.axis_index("y") + lax.axis_index("core"))
    count = received_ref.shape[0] // 8
    cols = received_ref.shape[-1]
    forward = lax.broadcasted_iota(jnp.int32, (8, 128), 0) < 3
    totals = [jnp.zeros((8, 128), f32)] * (cols // 128)
    runs = [jnp.zeros((8, 128), f32)] * (cols // 128)
    for q in range(count):
        gap = jnp.where(forward, near - q, q - near) - 1
        weight = tile_decay(gap, gap >= 0)
        to_edge = jnp.where(forward, math.exp(-(count - 1 - q) / 8.0), math.exp(-q / 8.0))
        for v in range(cols // 128):
            at = 8 * (q // 2 + 4 * (q % 2))
            value = received_ref[at : at + 8, 128 * v : 128 * v + 128]
            totals[v] = totals[v] + weight * value
            runs[v] = runs[v] + to_edge * value
    for v in range(cols // 128):
        at = slice(128 * v, 128 * v + 128)
        total_ref[:, at] = totals[v]
        for w in range(copies_ref.shape[0] // 8):
            copies_ref[8 * w : 8 * w + 8, at] = runs[v]


def short_kernel_body(scale, k_ref, c_ref, s_ref, ec_ref, held):
    cols = c_ref.shape[-1]
    for p in range(3):
        held[0:16, :] = c_ref[p]
        held[16:24, :] = jnp.zeros((8, cols), f32)
        for window in range(2):
            total = jnp.zeros((8, cols), f32)
            for b in range(5):
                part = jnp.zeros((8, cols), f32)
                for a in range(5):
                    start = 8 * window + a
                    part = part + k_ref[a, b] * held[start : start + 8, :]
                total = total + (part if b == 2 else shifted(part, b - 2))
            s_ref[p, 8 * window : 8 * window + 8, :] = total
    gap = lax.broadcasted_iota(jnp.int32, ec_ref.shape, 0) - lax.broadcasted_iota(jnp.int32, ec_ref.shape, 1)
    ec_ref[...] = jnp.exp(-jnp.abs(gap.astype(f32)) / scale)


def side_matrix(back):
    shape = (128, 128)
    i = lax.broadcasted_iota(jnp.int32, shape, 1 if back else 0)
    j = lax.broadcasted_iota(jnp.int32, shape, 0 if back else 1)
    return jnp.where(j // 8 == i, jnp.where(i < 8, 1.0, 0.0), 0.0)


def own_lane():
    shape = (8, 128)
    lane = lax.broadcasted_iota(jnp.int32, shape, 1)
    return (lane < 64) & (lane % 8 == lax.broadcasted_iota(jnp.int32, shape, 0))


def bend_kernel(decay, gain, s_ref, coarse_ref, total_ref, run_ref, ec_ref, sent_ref, pot_ref, rows, rim):
    cols = s_ref.shape[-1]
    e = decay
    near, far, tile = tile_place()
    near_count = 8
    forward = lax.broadcasted_iota(jnp.int32, (8, rows.shape[-1]), 0) < 3
    acc = total_ref[...]
    inside = jnp.where(forward, near, near_count - 1 - near)
    for w in range(run_ref.shape[0] // 8):
        gap = jnp.where(forward, far - w, w - far) - 1
        acc = acc + tile_decay(gap * near_count + inside, gap >= 0) * run_ref[8 * w : 8 * w + 8, :]
    c0, c1 = coarse_ref[0:3, :], coarse_ref[3:6, :]
    up, down = acc[0:3, :], acc[3:6, :]
    rows[12:16, :] = jnp.zeros((4, rows.shape[-1]), f32)
    rows[0:3, :] = e * c0 + e * e * c1 + e * e * down + up * (1.0 / e)
    rows[3:6, :] = c0 + e * c1 + up + e * down
    rows[6:9, :] = c1 + e * c0 + e * up + down
    rows[9:12, :] = e * e * c0 + e * c1 + e * e * up + down * (1.0 / e)
    smooth = gain * jnp.dot(rows[...], ec_ref[...], precision=highest, preferred_element_type=f32)
    stacked = jnp.concatenate([smooth[:, 128 * v : 128 * v + 128] for v in range(4)], axis=0)
    shape = (128, 512)
    group = lax.broadcasted_iota(jnp.int32, shape, 1) // 4
    grow = jnp.where(group == lax.broadcasted_iota(jnp.int32, shape, 0), 1.0, 0.0)
    grown = jnp.dot(stacked, grow, precision=highest, preferred_element_type=f32)
    long = jnp.concatenate([grown[16 * v : 16 * v + 16] for v in range(4)], axis=1)
    row = lax.broadcasted_iota(jnp.int32, (8, cols), 0)
    lane = lax.broadcasted_iota(jnp.int32, (8, cols), 1) % 128
    top = tile != 0
    bottom = tile != near_count * lax.axis_size("far") - 1
    rim[6:8, :] = jnp.zeros((2, cols), f32)
    side = jnp.zeros((8, cols), f32)
    for p in range(3):
        part = s_ref[p]
        wide = jnp.where(
            row < 4,
            jnp.broadcast_to(long[3 + p : 4 + p], (8, cols)),
            jnp.broadcast_to(long[6 + p : 7 + p], (8, cols)),
        )
        here = part[1:9] + wide
        above_row = jnp.where(top, part[0:1] + long[p : p + 1], 0.0)
        below_row = jnp.where(bottom, part[9:10] + long[9 + p : 10 + p], 0.0)
        pot_ref[p, 7:8, :] = above_row
        pot_ref[p, 8:16, :] = here
        pot_ref[p, 16:17, :] = below_row
        rim[p : p + 1, :] = above_row
        rim[3 + p : 4 + p, :] = below_row
        side = jnp.where(lane == 2 * p, shifted(here, -1 - 2 * p), side)
        side = jnp.where(lane == 2 * p + 1, shifted(here, 127 - 2 * p), side)
        for d in range(cols // 128):
            at = slice(128 * d, 128 * d + 128)
            sent_ref[4 * d + p] = here[:, at]
    rim_rows = rim[...]
    side = jnp.where(lane == 6, shifted(rim_rows, -7), side)
    side = jnp.where(lane == 7, shifted(rim_rows, 121), side)
    blocks = cols // 128
    spread = side_matrix(False)
    lined = jnp.concatenate([side[:, 128 * d : 128 * d + 128] for d in range(blocks)], axis=0)
    lined = jnp.dot(lined, spread, precision=highest, preferred_element_type=f32)
    own = own_lane()
    row = lax.broadcasted_iota(jnp.int32, (8, 128), 0)
    for d in range(blocks):
        line = jnp.sum(jnp.where(own, lined[8 * d : 8 * d + 8], 0.0), axis=0, keepdims=True)
        line = jnp.broadcast_to(line, (8, 128))
        sent_ref[4 * d + 3] = jnp.where(row == 6, line, rim_rows[:, 128 * d : 128 * d + 128])


def own_hessian(pot_ref, u_ref):
    cols = pot_ref.shape[-1]
    for p in range(3):
        here = pot_ref[p, 8:16, :]
        above, below = pot_ref[p, 7:15, :], pot_ref[p, 9:17, :]
        u11 = below - 2.0 * here + above
        u22 = shifted(here, 1) - 2.0 * here + shifted(here, -1)
        step = below - above
        u12 = (shifted(step, 1) - shifted(step, -1)) * 0.25
        for d in range(cols // 128):
            at = slice(128 * d, 128 * d + 128)
            u_ref[9 * d + 3 * p] = u11[:, at]
            u_ref[9 * d + 3 * p + 1] = u12[:, at]
            u_ref[9 * d + 3 * p + 2] = u22[:, at]


def advance(previous, current, u11, u12, u22, mixing, bending):
    kept = 1.0 - mixing
    bent = (
        u11 * current[0] + u12 * current[2],
        u11 * current[1] + u12 * current[3],
        u12 * current[0] + u22 * current[2],
        u12 * current[1] + u22 * current[3],
    )
    return tuple(kept * previous[i] + mixing * current[i] - bending * bent[i] for i in range(4))


def beside(value, left, right):
    lane = lax.broadcasted_iota(jnp.int32, value.shape, 1)
    before = jnp.where(lane == 0, jnp.broadcast_to(left, value.shape), pltpu.roll(value, 1, 1))
    after = jnp.where(lane == 127, jnp.broadcast_to(right, value.shape), pltpu.roll(value, 127, 1))
    return before, after


def over_rows(value, above, below):
    row = lax.broadcasted_iota(jnp.int32, value.shape, 0)
    before = jnp.where(row == 0, jnp.broadcast_to(above, value.shape), pltpu.roll(value, 1, 0))
    after = jnp.where(row == 7, jnp.broadcast_to(below, value.shape), pltpu.roll(value, 7, 0))
    return before, after


def scan_kernel(mixing_ref, bending_ref, sent_ref, pot_ref, state_ref, u_ref):
    own_hessian(pot_ref, u_ref)
    one = jnp.ones((8, 128), f32)
    zero = jnp.zeros((8, 128), f32)
    groups = sent_ref.shape[0] // 4
    own = own_lane()
    at = [(g % 4) * (groups // 4) + g // 4 for g in range(groups)]
    lines = [jnp.broadcast_to(sent_ref[4 * at[g] + 3, 6:7, :], (8, 128)) for g in range(groups)]
    lined = jnp.concatenate([jnp.where(own, line, 0.0) for line in lines], axis=0)
    sides = jnp.dot(lined, side_matrix(True), precision=highest, preferred_element_type=f32)

    previous = current = (one, zero, zero, one)
    for g in range(groups):
        for i in range(4):
            state_ref[8 * at[g] + i] = previous[i]
            state_ref[8 * at[g] + 4 + i] = current[i]
        rim = sent_ref[4 * at[g] + 3]
        side = sides[8 * g : 8 * g + 8]
        rim_left, rim_right = beside(rim, side[:, 6:7], side[:, 7:8])
        rim_step = rim_right - rim_left
        for p in range(3):
            k = 3 * g + p
            here = sent_ref[4 * at[g] + p]
            above, below = over_rows(here, rim[p : p + 1], rim[3 + p : 4 + p])
            left, right = beside(here, side[:, 2 * p : 2 * p + 1], side[:, 2 * p + 1 : 2 * p + 2])
            u11 = below - 2.0 * here + above
            u22 = right - 2.0 * here + left
            step_above, step_below = over_rows(right - left, rim_step[p : p + 1], rim_step[3 + p : 4 + p])
            u12 = (step_below - step_above) * 0.25
            later = advance(previous, current, u11, u12, u22, mixing_ref[k], bending_ref[k])
            previous, current = current, later


def final_kernel(mixing_ref, bending_ref, u_ref, state_ref, out_ref, held, sems):
    blocks = u_ref.shape[0] // 9
    first = 3 * (lax.axis_size("z") * lax.axis_index("x") + lax.axis_index("z"))
    copies = []
    for p in range(3):
        for d in range(blocks):
            at = slice(128 * d, 128 * d + 128)
            if p == 0:
                previous = tuple(state_ref[8 * d + i] for i in range(4))
                current = tuple(state_ref[8 * d + 4 + i] for i in range(4))
            else:
                current = tuple(held[p - 1, i, :, at] for i in range(4))
                if p == 1:
                    previous = tuple(state_ref[8 * d + 4 + i] for i in range(4))
                else:
                    previous = tuple(held[p - 2, i, :, at] for i in range(4))
            k = 9 * d + 3 * p
            later = advance(
                previous, current, u_ref[k], u_ref[k + 1], u_ref[k + 2], mixing_ref[first + p], bending_ref[first + p]
            )
            for i in range(4):
                held[p, i, :, at] = later[i]
        copy = pltpu.make_async_copy(held.at[p], out_ref.at[:, p], sems.at[p])
        copy.start()
        copies.append(copy)
    for copy in copies:
        copy.wait()


vmem = pl.BlockSpec(memory_space=pltpu.VMEM)
smem = pl.BlockSpec(memory_space=pltpu.SMEM)


def sds(*shape):
    return jax.ShapeDtypeStruct(shape, f32)


def call(kernel, name, n_smem, n_vmem, out_shape, scratch=(), cost=(0, 0, 0)):
    outs = jax.tree.map(lambda _: vmem, out_shape)
    return pl.pallas_call(
        kernel,
        name=name,
        out_shape=out_shape,
        in_specs=[smem] * n_smem + [vmem] * n_vmem,
        out_specs=outs,
        scratch_shapes=list(scratch),
        cost_estimate=pl.CostEstimate(flops=cost[0], bytes_accessed=cost[1], transcendentals=cost[2]),
        compiler_params=pltpu.CompilerParams(vmem_limit_bytes=24 << 20),
    )


def body(density, plane_slot, paint_weight, paint_bias, mix_weight, short_kernel):
    plane_count, row_count, col_count = density.shape
    tile = ("far", "y", "core")
    near_index = (2 * lax.axis_index("y") + lax.axis_index("core"))
    near_count, far_count = 8, lax.axis_size("far")
    tile_count = far_count * near_count
    group_count = lax.axis_size("x") * lax.axis_size("z")
    coarse_cols = col_count // 4
    row_scale = row_count * tile_count / 16.0
    col_scale = col_count / 16.0
    long_gain = 1.0 / math.sqrt(row_scale * col_scale)
    decay = math.exp(-1.0 / row_scale)

    even = near_index % 2 == 0
    last_rows, first_rows = density[:, 3:8, :], density[:, 0:5, :]
    pairs = [(i, i ^ 1) for i in range(tile_count)]
    mate = lax.ppermute(jnp.where(even, last_rows, first_rows), tile, pairs)
    pairs = [(i, ((i + 1) ^ 1) - 1) for i in range(1, tile_count - 1)]
    other = lax.ppermute(jnp.where(even, first_rows, last_rows), tile, pairs)

    scalars = jnp.concatenate([paint_bias, mix_weight])
    weights, pool = call(
        weights_kernel,
        "weights",
        2,
        0,
        (jax.ShapeDtypeStruct((channels * 8, 160), bf16), sds(col_count // 4, col_count // 16)),
        (),
        (10**6, 10**5, 0),
    )(paint_weight, scalars)
    mixing, bending = distances(plane_slot, 2 * plane_slot.shape[0])
    main, coarse, copies = call(
        functools.partial(paint_kernel, decay),
        "paint",
        1,
        5,
        (
            sds(plane_count, row_count, col_count),
            sds(8, coarse_cols),
            sds(8 * near_count, coarse_cols),
        ),
        [pltpu.VMEM((16, col_count), f32), pltpu.VMEM((160, col_count), bf16), pltpu.VMEM((8, col_count), f32)],
        (4 * 10**9, 2 * 10**6, 10**6),
    )(scalars, density, mate, other, weights, pool)
    copies, mixing, bending = lax.optimization_barrier((copies, mixing, bending))

    received = lax.all_to_all(copies, ("core", "y"), 0, 0, tiled=True)
    convergence = call(
        edge_kernel,
        "edges",
        1,
        5,
        sds(plane_count, 16, col_count),
        [pltpu.VMEM((16, col_count), f32), pltpu.VMEM((160, col_count), bf16)],
        (8 * 10**9, 2 * 10**6, 10**6),
    )(scalars, density, mate, other, weights, main)
    total, run_copies = call(
        runs_kernel, "runs", 0, 1, (sds(8, coarse_cols), sds(8 * far_count, coarse_cols)), (), (10**6, 10**5, 0)
    )(received)
    convergence, run_copies = lax.optimization_barrier((convergence, run_copies))
    runs = lax.all_to_all(run_copies, "far", 0, 0, tiled=True)
    short_part, col_kernel = call(
        functools.partial(short_kernel_body, col_scale),
        "short",
        1,
        1,
        (sds(plane_count, 16, col_count), sds(coarse_cols, coarse_cols)),
        [pltpu.VMEM((24, col_count), f32)],
        (10**7, 10**6, 0),
    )(short_kernel, convergence)

    sent, potential = call(
        functools.partial(bend_kernel, decay, long_gain),
        "bend",
        0,
        5,
        (sds(group_count * 4, 8, 128), sds(plane_count, 24, col_count)),
        [pltpu.VMEM((16, coarse_cols), f32), pltpu.VMEM((8, col_count), f32)],
        (10**8, 2 * 10**6, 0),
    )(short_part, coarse, total, runs, col_kernel)

    gathered = lax.all_to_all(sent, ("z", "x"), 0, 0, tiled=True)
    states, shear = call(
        scan_kernel,
        "scan",
        2,
        2,
        (sds(group_count * 8, 8, 128), sds(group_count * 9, 8, 128)),
        (),
        (10**7, 10**6, 0),
    )(mixing, bending, gathered, potential)
    mine = lax.all_to_all(states, ("z", "x"), 0, 0, tiled=True)
    return pl.pallas_call(
        final_kernel,
        name="final",
        out_shape=sds(4, plane_count, row_count, col_count),
        in_specs=[smem, smem, vmem, vmem],
        out_specs=pl.BlockSpec(memory_space=pl.ANY),
        scratch_shapes=[pltpu.VMEM((plane_count, 4, row_count, col_count), f32), pltpu.SemaphoreType.DMA((3,))],
        cost_estimate=pl.CostEstimate(flops=10**7, bytes_accessed=10**6, transcendentals=0),
        compiler_params=pltpu.CompilerParams(vmem_limit_bytes=24 << 20),
    )(mixing, bending, shear, mine)


def solution(mesh):
    planes, tiles = mesh.devices.shape
    split = Mesh(mesh.devices.reshape(planes // 4, 4, 4, tiles // 8, 2), ("x", "z", "far", "y", "core"))
    tile = ("far", "y", "core")
    plane = ("x", "z")
    placed = (P(plane, tile, None), P(), P(), P(), P(), P())
    return jax.shard_map(
        body, mesh=split, in_specs=placed, out_specs=P(None, plane, tile, None), check_vma=False
    )
```
